32 devices in a mesh: mem: 8 (over y, x, core), reg: 4 (over z).
Axes of the slice: x: 2, y: 2, z: 4, core: 2. Of those that a mesh axis runs over, the one named last changes fastest.
Arguments:
- sample_stack: float32 [64, 11, 8, 256], P('mem', None, 'reg'), may hold values from -6 to 6
- weights: float32 [4, 64], P('reg', 'mem'), may hold values from 0.1 to 10
- offspring: int32 [4, 64], P('reg'), may hold values from 0 to 63
- localize: float32 [8, 256], P('reg'), may hold values from 0.2 to 0.9
Outputs:
- posterior: float32 [64, 11, 8, 256], P('mem', None, 'reg')
The draws below stay inside these ranges and needn't reach their ends.
Inputs may be any that keep to these rules, and one draw needn't show every extreme that they name: `offspring`: each entry names a member.
All inputs are finite; a program needn't handle non-finite values.
Results may differ from the reference program's by a relative error of at most 0.0021.
Values may be sent and summed in bfloat16 or wider, within the bound.
A program may use at most 64 MiB of HBM per device.

```python
import math
import jax
import jax.numpy as jnp
import numpy as np
from jax import lax

VERTICAL_QUANTS = 11
BAND_LATITUDES = 2
LATTICE_WIDTH = 256
SAMPLE_TOTAL = 64
ZONE_BANDS_NUM = 4
NY = 8


def with_ends(values, rng, least, high):
    spot = [jax.random.randint(jax.random.fold_in(rng, axis), (), 0, length) for axis, length in enumerate(values.shape)]
    longest = values.shape.index(max(values.shape))
    next_to = spot[:longest] + [(spot[longest] + 1) % values.shape[longest]] + spot[longest + 1:]
    return values.at[tuple(spot)].set(least).at[tuple(next_to)].set(high)


def block_scale(stream_key, dims, split, smallest, largest):
    def one(dim, shards_of):
        steps = jax.random.uniform(jax.random.fold_in(jax.random.fold_in(stream_key, 6), dim), (shards_of,), jnp.float32, smallest / len(split), largest / len(split))
        return jnp.repeat(jnp.exp(steps), dims[dim] // shards_of).reshape((-1,) + (1,) * (len(dims) - dim - 1))

    factor_of = one(*split[0])
    for cut in split[1:]:
        factor_of = factor_of * one(*cut)
    return factor_of


def cumulative_ranks(count, slope):
    portions = [(1 << 20) // math.isqrt(grade ** slope) + 1 for grade in range(1, count + 1)]
    width = 1 + sum(portions) // (1 << 30)
    return np.cumsum(np.array([max(1, weight // width) for weight in portions]))


def skewed_ids(stream_key, shape, number_of, skew):
    table = cumulative_ranks(number_of, skew)
    pick = jax.random.randint(jax.random.fold_in(stream_key, 1), shape, 0, int(table[number_of - 1]))
    standing = jnp.searchsorted(jnp.asarray(table, jnp.int32), pick, side="right")
    return jax.random.permutation(jax.random.fold_in(stream_key, 2), number_of)[standing].astype(jnp.int32)


def noise(stream_key, dims, scale, reach, pieces=(), dtype=jnp.bfloat16):
    values = jax.random.normal(stream_key, dims, jnp.float32) * scale
    if len(pieces) > 0:
        values = block_scale(stream_key, dims, pieces, -0.22, 0.18) * values
    return jnp.clip(values, min=-reach, max=reach).astype(dtype)


def setup_inputs(seed: int = 0) -> dict:
    key_list = jax.random.split(jax.random.key(seed), 5)
    return {
        "sample_stack": noise(key_list[0], (SAMPLE_TOTAL, VERTICAL_QUANTS, NY, LATTICE_WIDTH), 1.0, 6.0, ((0, 8), (2, 4)), jnp.float32),
        "weights": jnp.clip(jnp.exp(math.log(10.0) - 4.6051702 * jax.random.uniform(key_list[1], (ZONE_BANDS_NUM, SAMPLE_TOTAL), jnp.float32) ** block_scale(key_list[1], (ZONE_BANDS_NUM, SAMPLE_TOTAL), ((0, 4), (1, 8)), -0.2, 0.2)), 0.1, 10.0),
        "offspring": with_ends(skewed_ids(key_list[2], (ZONE_BANDS_NUM, SAMPLE_TOTAL), SAMPLE_TOTAL, 2), jax.random.fold_in(key_list[2], 3), 0, SAMPLE_TOTAL - 1).astype(jnp.int32),
        "localize": jnp.clip(0.2 + 0.7 * jax.random.uniform(key_list[3], (NY, LATTICE_WIDTH), jnp.float32) ** block_scale(key_list[3], (NY, LATTICE_WIDTH), ((0, 4),), -0.2, 0.2), 0.2, 0.9),
    }


wave_gain = 0.25
advect_gain = 0.1
diffuse_gain = 0.1
small_eps = 1e-05

def advance(padded):
    centre = padded[:, :, 1:-1]
    upper_rows = padded[:, :, 2:]
    lower_rows = padded[:, :, :-2]
    right_cols = jnp.roll(centre, -1, 3)
    left_cols = jnp.roll(centre, 1, 3)
    slope_east = 0.5 * (right_cols - left_cols)
    slope_north = 0.5 * (upper_rows - lower_rows)
    laplace = right_cols + left_cols + upper_rows + lower_rows - 4.0 * centre
    height = centre[:, 0]
    flow_east = centre[:, 1]
    flow_north = centre[:, 2]
    tracer = centre[:, 3:]
    new_height = height - wave_gain * (slope_east[:, 1] + slope_north[:, 2])
    new_east = flow_east - wave_gain * slope_east[:, 0]
    new_north = flow_north - wave_gain * slope_north[:, 0]
    new_tracer = tracer - advect_gain * (flow_east[:, None] * slope_east[:, 3:] + flow_north[:, None] * slope_north[:, 3:]) + diffuse_gain * laplace[:, 3:]
    return jnp.concatenate([new_height[:, None], new_east[:, None], new_north[:, None], new_tracer], axis=1)

def propagate_dynamics(model_snapshot):
    padded = jnp.concatenate([model_snapshot[:, :, -1:], model_snapshot, model_snapshot[:, :, :1]], axis=2)
    return advance(padded)

def reference(sample_stack, weights, offspring, localize):
    background_prediction = propagate_dynamics(propagate_dynamics(sample_stack))
    band_partition = background_prediction.reshape(SAMPLE_TOTAL, VERTICAL_QUANTS, ZONE_BANDS_NUM, BAND_LATITUDES, LATTICE_WIDTH)
    importance_factors = jnp.transpose(weights)[:, None, :, None, None]
    weight_total = lax.optimization_barrier(jnp.sum(weights, axis=1))[None, :, None, None]
    sample_average_map = lax.optimization_barrier(jnp.sum(importance_factors * band_partition, axis=0)) / weight_total
    variance = lax.optimization_barrier(jnp.sum(importance_factors * (band_partition - sample_average_map) ** 2, axis=0)) / weight_total
    rounded = lax.optimization_barrier(band_partition.astype(jnp.bfloat16)).astype(jnp.float32)
    sources = jnp.transpose(rounded, (2, 0, 1, 3, 4))
    picked = jnp.take_along_axis(sources, offspring.astype(jnp.int32)[:, :, None, None, None], axis=1)
    sample_duplicates = jnp.transpose(picked, (1, 2, 0, 3, 4))
    cell_weight_value = localize.reshape(ZONE_BANDS_NUM, BAND_LATITUDES, LATTICE_WIDTH)[None, None]
    spread_offset = cell_weight_value * (sample_duplicates - sample_average_map) + (1.0 - cell_weight_value) * (band_partition - sample_average_map)
    spread = lax.optimization_barrier(jnp.mean(spread_offset * spread_offset, axis=0))
    scale_ratio = jnp.sqrt((variance + small_eps) / (spread + small_eps))
    posterior = sample_average_map + scale_ratio * spread_offset
    return posterior.reshape(SAMPLE_TOTAL, VERTICAL_QUANTS, NY, LATTICE_WIDTH)
```

```python
import functools

import jax
import jax.numpy as jnp
from jax import lax
from jax.experimental import pallas as pl
from jax.experimental.pallas import tpu as pltpu
from jax.sharding import PartitionSpec as P

MESH = pl.DeviceIdType.MESH
wave_gain = 0.25
advect_gain = 0.1
diffuse_gain = 0.1
small_eps = 1e-05
LANES = 128
FLOWS = 3
STATS = 16


def field_groups(fields, halves, n):
    size = max(FLOWS, n // halves)
    groups, first, slot = [], 0, 0
    while first < fields:
        last = min(fields, first + size)
        per = -(-(last - first) * halves // n)
        groups.append((first, last, slot, per))
        first, slot = last, slot + per
    return groups, slot


def sideways(block):
    width = block.shape[-1]
    return pltpu.roll(block, width - 1, 1), pltpu.roll(block, 1, 1)


def flow_step(height, east, north, rows):
    half = 0.5 * wave_gain
    new_height, new_east, new_north = {}, {}, {}
    for r in rows:
        e_right, e_left = sideways(east[r])
        h_right, h_left = sideways(height[r])
        new_height[r] = height[r] - half * ((e_right - e_left) + (north[r + 1] - north[r - 1]))
        new_east[r] = east[r] - half * (h_right - h_left)
        new_north[r] = north[r] - half * (height[r + 1] - height[r - 1])
    return new_height, new_east, new_north


def tracer_gains(east, north, rows):
    gains = {}
    for r in rows:
        e, v = (0.5 * advect_gain) * east[r], (0.5 * advect_gain) * north[r]
        gains[r] = (diffuse_gain - e, diffuse_gain + e, diffuse_gain - v, diffuse_gain + v)
    return gains


def tracer_step(tracer, gains, rows):
    new = {}
    for r in rows:
        right, left = sideways(tracer[r])
        g_right, g_left, g_up, g_low = gains[r]
        new[r] = (
            (1.0 - 4.0 * diffuse_gain) * tracer[r]
            + (g_right * right + g_left * left)
            + (g_up * tracer[r + 1] + g_low * tracer[r - 1])
        )
    return new


def kernel(
    n, regs, groups, fields, rows, halves, members,
    x_hbm, w_hbm, off_hbm, loc_hbm, out_ref,
    xs, w_ref, off_ref, loc_ref, own, halo, cast, sendb, recv, retb, got, wide, locs, pick,
    load_sem, halo_send, halo_recv, w_send, w_recv, to_send, to_recv, back_send, back_recv,
):
    me = lax.axis_index("mem")
    band = lax.axis_index("reg")
    stride = fields * halves * rows
    pair = rows * members
    everyone = n * members

    loads = []
    for i, (src, dst) in enumerate(((x_hbm, xs), (w_hbm, w_ref), (off_hbm, off_ref), (loc_hbm, loc_ref))):
        copy = pltpu.make_async_copy(src, dst, load_sem.at[i])
        copy.start()
        loads.append(copy)

    edge = lax.rem(band + regs - 1, regs) // (regs - 1)
    ways = (
        (lax.rem(band + 1 + edge * (regs - 2), regs), edge),
        (lax.rem(band + regs - 1 - edge * (regs - 2), regs), 1 - edge),
    )
    barrier = pltpu.get_barrier_semaphore()
    for target, _ in ways:
        pl.semaphore_signal(barrier, inc=1, device_id={"reg": target}, device_id_type=MESH)
    for o in range(1, n):
        pl.semaphore_signal(barrier, inc=1, device_id={"mem": lax.rem(me + o, n)}, device_id_type=MESH)

    def place(f, c, r):
        return pl.ds((f * halves + c) * rows + r, members, stride=stride)

    loads[0].wait()
    for f in range(fields):
        for c in range(halves):
            own[f, c] = jnp.concatenate([xs[place(f, c, r), :] for r in range(rows)], axis=0).astype(own.dtype)
    pl.semaphore_wait(barrier, n + 1)

    halos = [[] for _ in groups]
    for target, way in ways:
        for g, (first, last, _, _) in enumerate(groups):
            copy = pltpu.make_async_remote_copy(
                src_ref=own.at[first:last], dst_ref=halo.at[way, first:last],
                send_sem=halo_send.at[way, g], recv_sem=halo_recv.at[way, g],
                device_id={"reg": target}, device_id_type=MESH,
            )
            copy.start()
            halos[g].append(copy)

    loads[1].wait()
    eye = lax.broadcasted_iota(jnp.int32, (members, members), 0) == lax.broadcasted_iota(
        jnp.int32, (members, members), 1
    )
    column = jnp.sum(jnp.where(eye, jnp.broadcast_to(w_ref[...], (members, members)), 0.0), axis=1, keepdims=True)
    one = jnp.broadcast_to(column, (members, LANES))
    wide[me] = jnp.concatenate([one] * rows, axis=0)
    weights_out = []
    for o in range(1, n):
        copy = pltpu.make_async_remote_copy(
            src_ref=wide.at[me], dst_ref=wide.at[me], send_sem=w_send.at[o - 1], recv_sem=w_recv.at[o - 1],
            device_id={"mem": lax.rem(me + o, n)}, device_id_type=MESH,
        )
        copy.start()
        weights_out.append(copy)

    loads[2].wait()
    block = n * pair
    j_row = lax.broadcasted_iota(jnp.int32, (block, everyone), 0)
    wanted = (j_row // pair) * members + lax.rem(j_row, members)
    chosen = lax.broadcasted_iota(jnp.int32, (block, everyone), 1) == wanted
    source = jnp.sum(
        jnp.where(chosen, jnp.broadcast_to(off_ref[...].astype(jnp.float32), (block, everyone)), 0.0),
        axis=1, keepdims=True,
    ).astype(jnp.int32)
    row = lax.broadcasted_iota(jnp.int32, (block, 1), 0)
    target_row = (source // members) * pair + lax.rem(row // members, rows) * members + lax.rem(source, members)
    k_col = lax.broadcasted_iota(jnp.int32, (block, block), 1)
    pick[...] = (k_col == jnp.broadcast_to(target_row, (block, block))).astype(jnp.float32).astype(pick.dtype)

    loads[3].wait()
    for c in range(halves):
        locs[c] = jnp.concatenate(
            [
                jnp.broadcast_to(loc_ref[r:r + 1, c * LANES:(c + 1) * LANES], (members, LANES))
                for r in range(rows)
            ],
            axis=0,
        )
    for g, (first, last, slot, per) in enumerate(groups):
        for b in range((last - first) * halves, n * per):
            sendb[b % n, slot + b // n] = jnp.zeros((pair, LANES), sendb.dtype)

    inner, outer = range(rows), range(-1, rows + 1)
    gains = []
    outgoing = [[] for _ in groups]
    for g, (first, last, slot, per) in enumerate(groups):
        for copy in halos[g]:
            copy.wait_recv()

        def column_of(f):
            values = {}
            for way, base in ((0, -rows), (1, rows)):
                both = [halo[way, f, c].astype(jnp.float32) for c in range(halves)]
                for r in range(rows):
                    values[base + r] = jnp.concatenate([b[r * members:(r + 1) * members] for b in both], axis=1)
            for r in range(rows):
                values[r] = jnp.concatenate([xs[place(f, c, r), :] for c in range(halves)], axis=1)
            return values

        done = {}
        if g == 0:
            height, east, north = (column_of(f) for f in range(FLOWS))
            gains.append(tracer_gains(east, north, outer))
            flow = flow_step(height, east, north, outer)
            gains.append(tracer_gains(flow[1], flow[2], inner))
            for f, value in enumerate(flow_step(*flow, inner)):
                done[f] = value
        for f in range(max(first, FLOWS), last):
            done[f] = tracer_step(tracer_step(column_of(f), gains[0], outer), gains[1], inner)
        for f in range(first, last):
            for c in range(halves):
                both = jnp.concatenate([done[f][r][:, c * LANES:(c + 1) * LANES] for r in inner], axis=0)
                cast[f, c] = both
                b = (f - first) * halves + c
                sendb[b % n, slot + b // n] = both.astype(sendb.dtype)
        for o in range(1, n):
            peer = lax.rem(me + o, n)
            copy = pltpu.make_async_remote_copy(
                src_ref=sendb.at[peer, slot:slot + per], dst_ref=recv.at[me, slot:slot + per],
                send_sem=to_send.at[g, o - 1], recv_sem=to_recv.at[g, o - 1],
                device_id={"mem": peer}, device_id_type=MESH,
            )
            copy.start()
            outgoing[g].append(copy)
        for s in range(slot, slot + per):
            recv[me, s] = sendb[me, s]

    for copy in weights_out:
        copy.wait_recv()
    weight = wide[...].reshape(n, rows, members, LANES)
    inverse = 1.0 / jnp.sum(weight, axis=(0, 2), keepdims=True)[0]

    returned = [[] for _ in groups]
    for g, (first, last, slot, per) in enumerate(groups):
        for copy in outgoing[g]:
            copy.wait_recv()
        for s in range(slot, slot + per):
            low_bits = recv[:, s].reshape(block, LANES)
            copies = lax.dot_general(
                pick[...], low_bits, (((1,), (0,)), ((), ())), preferred_element_type=jnp.float32
            )
            value = low_bits.astype(jnp.float32).reshape(n, rows, members, LANES)
            mean = jnp.sum(jnp.sum(weight * value, axis=0), axis=1, keepdims=True) * inverse
            departure = value - mean[None]
            variance = jnp.sum(jnp.sum(weight * departure * departure, axis=0), axis=1, keepdims=True) * inverse
            local = locs[lax.rem((s - slot) * n + me, halves)].reshape(1, rows, members, LANES)
            drawn = copies.reshape(n, rows, members, LANES)
            deviation = local * (drawn - mean[None]) + (1.0 - local) * departure
            spread = jnp.sum(jnp.sum(deviation * deviation, axis=0), axis=1, keepdims=True) / everyone
            ratio = jnp.sqrt((variance + small_eps) / (spread + small_eps))
            known = jnp.concatenate([mean[r] for r in range(rows)] + [ratio[r] for r in range(rows)], axis=0)
            coarse = known.astype(jnp.bfloat16).astype(jnp.float32)
            known = jnp.concatenate(
                [coarse, known - coarse, jnp.zeros((STATS - 4 * rows, LANES), jnp.float32)], axis=0
            ).astype(retb.dtype)
            low_copies = copies.astype(retb.dtype).reshape(n, pair, LANES)
            for d in range(n):
                retb[d, s, :pair] = low_copies[d]
                retb[d, s, pair:] = known
        for o in range(1, n):
            peer = lax.rem(me + o, n)
            copy = pltpu.make_async_remote_copy(
                src_ref=retb.at[peer, slot:slot + per], dst_ref=got.at[me, slot:slot + per],
                send_sem=back_send.at[g, o - 1], recv_sem=back_recv.at[g, o - 1],
                device_id={"mem": peer}, device_id_type=MESH,
            )
            copy.start()
            returned[g].append(copy)
        for s in range(slot, slot + per):
            got[me, s] = retb[me, s]

    for g, (first, last, slot, per) in enumerate(groups):
        for copy in returned[g]:
            copy.wait_recv()
        for f in range(first, last):
            for c in range(halves):
                b = (f - first) * halves + c
                block_in = got[b % n, slot + b // n].astype(jnp.float32)
                known = block_in[pair:pair + 2 * rows] + block_in[pair + 2 * rows:pair + 4 * rows]
                forecast = cast[f, c]
                for r in range(rows):
                    part = slice(r * members, (r + 1) * members)
                    mean, ratio = known[r:r + 1], known[rows + r:rows + r + 1]
                    local = locs[c, part]
                    deviation = local * (block_in[part] - mean) + (1.0 - local) * (forecast[part] - mean)
                    out_ref[place(f, c, r), :] = mean + ratio * deviation

    for copies_out in halos + [weights_out] + outgoing + returned:
        for copy in copies_out:
            copy.wait_send()


def solution(mesh):
    n, regs = mesh.shape["mem"], mesh.shape["reg"]

    def per_device(sample_stack, weights, offspring, localize):
        members, fields, rows, width = sample_stack.shape
        halves = width // LANES
        groups, slots = field_groups(fields, halves, n)
        count = len(groups)
        pair = rows * members
        x = sample_stack.reshape(members, fields, rows, halves, LANES).transpose(0, 1, 3, 2, 4)
        x = x.reshape(members * fields * halves * rows, LANES)
        hbm = pl.BlockSpec(memory_space=pltpu.HBM)
        vmem = pltpu.VMEM
        sem = pltpu.SemaphoreType.DMA
        f32, b16 = jnp.float32, jnp.bfloat16
        out = pl.pallas_call(
            functools.partial(kernel, n, regs, groups, fields, rows, halves, members),
            out_shape=jax.ShapeDtypeStruct(x.shape, f32),
            in_specs=[hbm] * 4,
            out_specs=pl.BlockSpec(memory_space=vmem),
            scratch_shapes=[
                vmem(x.shape, f32),
                vmem(weights.shape, f32),
                vmem(offspring.shape, jnp.int32),
                vmem(localize.shape, f32),
                vmem((fields, halves, pair, LANES), b16),
                vmem((2, fields, halves, pair, LANES), b16),
                vmem((fields, halves, pair, LANES), f32),
                vmem((n, slots, pair, LANES), b16),
                vmem((n, slots, pair, LANES), b16),
                vmem((n, slots, pair + STATS, LANES), b16),
                vmem((n, slots, pair + STATS, LANES), b16),
                vmem((n, pair, LANES), f32),
                vmem((halves, pair, LANES), f32),
                vmem((n * pair, n * pair), b16),
                sem((4,)), sem((2, count)), sem((2, count)), sem((n - 1,)), sem((n - 1,)),
                sem((count, n - 1)), sem((count, n - 1)), sem((count, n - 1)), sem((count, n - 1)),
            ],
            compiler_params=pltpu.CompilerParams(
                collective_id=0, has_side_effects=True, vmem_limit_bytes=32 << 20
            ),
        )(*(pltpu.with_memory_space_constraint(a, pltpu.HBM) for a in (x, weights, offspring, localize)))
        out = out.reshape(members, fields, halves, rows, LANES).transpose(0, 1, 3, 2, 4)
        return out.reshape(members, fields, rows, width)

    in_specs = (P("mem", None, "reg", None), P("reg", "mem"), P("reg", None), P("reg", None))
    return jax.shard_map(
        per_device, mesh=mesh, in_specs=in_specs, out_specs=P("mem", None, "reg", None), check_vma=False
    )
```

```python
import functools

import jax
import jax.numpy as jnp
from jax import lax
from jax.experimental import pallas as pl
from jax.experimental.pallas import tpu as pltpu
from jax.sharding import PartitionSpec as P

MESH = pl.DeviceIdType.MESH
wave_gain = 0.25
advect_gain = 0.1
diffuse_gain = 0.1
small_eps = 1e-05
LANES = 128
FLOWS = 3
STATS = 16


def field_groups(fields, halves, n):
    size = max(FLOWS, n // halves)
    groups, first, slot = [], 0, 0
    while first < fields:
        last = min(fields, first + size)
        per = -(-(last - first) * halves // n)
        groups.append((first, last, slot, per))
        first, slot = last, slot + per
    return groups, slot


def settle(ref, semaphore):
    pltpu.make_async_copy(ref, ref, semaphore).wait()


def sideways(block):
    width = block.shape[-1]
    return pltpu.roll(block, width - 1, 1), pltpu.roll(block, 1, 1)


def flow_step(height, east, north, rows):
    half = 0.5 * wave_gain
    new_height, new_east, new_north = {}, {}, {}
    for r in rows:
        e_right, e_left = sideways(east[r])
        h_right, h_left = sideways(height[r])
        new_height[r] = height[r] - half * ((e_right - e_left) + (north[r + 1] - north[r - 1]))
        new_east[r] = east[r] - half * (h_right - h_left)
        new_north[r] = north[r] - half * (height[r + 1] - height[r - 1])
    return new_height, new_east, new_north


def tracer_gains(east, north, rows):
    gains = {}
    for r in rows:
        e, v = (0.5 * advect_gain) * east[r], (0.5 * advect_gain) * north[r]
        gains[r] = (diffuse_gain - e, diffuse_gain + e, diffuse_gain - v, diffuse_gain + v)
    return gains


def tracer_step(tracer, gains, rows):
    new = {}
    for r in rows:
        right, left = sideways(tracer[r])
        g_right, g_left, g_up, g_low = gains[r]
        new[r] = (
            (1.0 - 4.0 * diffuse_gain) * tracer[r]
            + (g_right * right + g_left * left)
            + (g_up * tracer[r + 1] + g_low * tracer[r - 1])
        )
    return new


def kernel(
    n, regs, groups, fields, rows, halves, members,
    x_hbm, w_hbm, off_hbm, loc_hbm, out_ref,
    xs, w_ref, off_ref, loc_ref, own, halo, cast, sendb, recv, retb, got, wide, locs, pick,
    own_sem, halo_recv, to_recv, back_recv, w_recv, ready,
):
    me = lax.axis_index("mem")
    band = lax.axis_index("reg")
    stride = fields * halves * rows
    pair = rows * members
    everyone = n * members

    loads = []
    for i, (src, dst) in enumerate(((x_hbm, xs), (w_hbm, w_ref), (off_hbm, off_ref), (loc_hbm, loc_ref))):
        copy = pltpu.make_async_copy(src, dst, own_sem.at[i])
        copy.start()
        loads.append(copy)

    edge = lax.rem(band + regs - 1, regs) // (regs - 1)
    ways = (
        (lax.rem(band + 1 + edge * (regs - 2), regs), edge),
        (lax.rem(band + regs - 1 - edge * (regs - 2), regs), 1 - edge),
    )
    last_band = band // (regs - 1)
    relay_band = lax.rem(band + 1, regs) // (regs - 1)
    barrier = pltpu.get_barrier_semaphore()
    for target, _ in ways:
        pl.semaphore_signal(barrier, inc=1, device_id={"reg": target}, device_id_type=MESH)
    for o in range(1, n):
        pl.semaphore_signal(
            barrier, inc=1, device_id={"mem": lax.rem(me + o, n), "reg": band - last_band}, device_id_type=MESH
        )

    def place(f, c, r):
        return pl.ds((f * halves + c) * rows + r, members, stride=stride)

    loads[0].wait()
    for f in range(fields):
        for c in range(halves):
            own[f, c] = jnp.concatenate([xs[place(f, c, r), :] for r in range(rows)], axis=0).astype(own.dtype)
    pl.semaphore_wait(barrier, 2 + (n - 1) * (1 - last_band + relay_band))

    @pl.when(relay_band == 1)
    def _():
        pl.semaphore_signal(ready, inc=1, device_id={"reg": lax.rem(band + 1, regs)}, device_id_type=MESH)

    for target, way in ways:
        for g, (first, last, _, _) in enumerate(groups):
            copy = pltpu.make_async_remote_copy(
                src_ref=own.at[first:last], dst_ref=halo.at[way, first:last],
                send_sem=own_sem.at[0], recv_sem=halo_recv.at[g],
                device_id={"reg": target}, device_id_type=MESH,
            )
            copy.start()

    loads[2].wait()
    block = n * pair
    j_row = lax.broadcasted_iota(jnp.int32, (block, everyone), 0)
    wanted = (j_row // pair) * members + lax.rem(j_row, members)
    chosen = lax.broadcasted_iota(jnp.int32, (block, everyone), 1) == wanted
    source = jnp.sum(
        jnp.where(chosen, jnp.broadcast_to(off_ref[...].astype(jnp.float32), (block, everyone)), 0.0),
        axis=1, keepdims=True,
    ).astype(jnp.int32)
    row = lax.broadcasted_iota(jnp.int32, (block, 1), 0)
    target_row = (source // members) * pair + lax.rem(row // members, rows) * members + lax.rem(source, members)
    k_col = lax.broadcasted_iota(jnp.int32, (block, block), 1)
    pick[...] = (k_col == jnp.broadcast_to(target_row, (block, block))).astype(jnp.float32).astype(pick.dtype)

    loads[3].wait()
    for c in range(halves):
        locs[c] = jnp.concatenate(
            [
                jnp.broadcast_to(loc_ref[r:r + 1, c * LANES:(c + 1) * LANES], (members, LANES))
                for r in range(rows)
            ],
            axis=0,
        )
    for g, (first, last, slot, per) in enumerate(groups):
        for b in range((last - first) * halves, n * per):
            sendb[b % n, slot + b // n] = jnp.zeros((pair, LANES), sendb.dtype)

    @pl.when(last_band == 1)
    def _():
        pl.semaphore_wait(ready, 1)

    loads[1].wait()
    eye = lax.broadcasted_iota(jnp.int32, (members, members), 0) == lax.broadcasted_iota(
        jnp.int32, (members, members), 1
    )
    column = jnp.sum(jnp.where(eye, jnp.broadcast_to(w_ref[...], (members, members)), 0.0), axis=1, keepdims=True)
    wide[me] = jnp.broadcast_to(column, (members, LANES))
    for o in range(1, n):
        copy = pltpu.make_async_remote_copy(
            src_ref=wide.at[me], dst_ref=wide.at[me], send_sem=own_sem.at[1], recv_sem=w_recv,
            device_id={"mem": lax.rem(me + o, n)}, device_id_type=MESH,
        )
        copy.start()

    inner, outer = range(rows), range(-1, rows + 1)
    gains = []
    for g, (first, last, slot, per) in enumerate(groups):
        settle(halo.at[:, first:last], halo_recv.at[g])

        def column_of(f):
            values = {}
            for way, base in ((0, -rows), (1, rows)):
                both = [halo[way, f, c].astype(jnp.float32) for c in range(halves)]
                for r in range(rows):
                    values[base + r] = jnp.concatenate([b[r * members:(r + 1) * members] for b in both], axis=1)
            for r in range(rows):
                values[r] = jnp.concatenate([xs[place(f, c, r), :] for c in range(halves)], axis=1)
            return values

        done = {}
        if g == 0:
            height, east, north = (column_of(f) for f in range(FLOWS))
            gains.append(tracer_gains(east, north, outer))
            flow = flow_step(height, east, north, outer)
            gains.append(tracer_gains(flow[1], flow[2], inner))
            for f, value in enumerate(flow_step(*flow, inner)):
                done[f] = value
        for f in range(max(first, FLOWS), last):
            done[f] = tracer_step(tracer_step(column_of(f), gains[0], outer), gains[1], inner)
        for f in range(first, last):
            for c in range(halves):
                both = jnp.concatenate([done[f][r][:, c * LANES:(c + 1) * LANES] for r in inner], axis=0)
                cast[f, c] = both
                b = (f - first) * halves + c
                sendb[b % n, slot + b // n] = both.astype(sendb.dtype)
        for o in range(1, n):
            peer = lax.rem(me + o, n)
            copy = pltpu.make_async_remote_copy(
                src_ref=sendb.at[peer, slot:slot + per], dst_ref=recv.at[me, slot:slot + per],
                send_sem=own_sem.at[2], recv_sem=to_recv.at[g],
                device_id={"mem": peer}, device_id_type=MESH,
            )
            copy.start()
        for s in range(slot, slot + per):
            recv[me, s] = sendb[me, s]

    settle(wide.at[:n - 1], w_recv)
    weight = wide[...].reshape(n, 1, members, LANES)
    inverse = 1.0 / jnp.sum(jnp.sum(weight, axis=0), axis=1, keepdims=True)

    for g, (first, last, slot, per) in enumerate(groups):
        settle(recv.at[:n - 1, slot:slot + per], to_recv.at[g])
        for s in range(slot, slot + per):
            low_bits = recv[:, s].reshape(block, LANES)
            copies = lax.dot_general(
                pick[...], low_bits, (((1,), (0,)), ((), ())), preferred_element_type=jnp.float32
            )
            value = low_bits.astype(jnp.float32).reshape(n, rows, members, LANES)
            mean = jnp.sum(jnp.sum(weight * value, axis=0), axis=1, keepdims=True) * inverse
            departure = value - mean[None]
            variance = jnp.sum(jnp.sum(weight * departure * departure, axis=0), axis=1, keepdims=True) * inverse
            local = locs[lax.rem((s - slot) * n + me, halves)].reshape(1, rows, members, LANES)
            drawn = copies.reshape(n, rows, members, LANES)
            deviation = local * (drawn - mean[None]) + (1.0 - local) * departure
            spread = jnp.sum(jnp.sum(deviation * deviation, axis=0), axis=1, keepdims=True) / everyone
            ratio = jnp.sqrt((variance + small_eps) / (spread + small_eps))
            known = jnp.concatenate([mean[r] for r in range(rows)] + [ratio[r] for r in range(rows)], axis=0)
            coarse = known.astype(jnp.bfloat16).astype(jnp.float32)
            known = jnp.concatenate(
                [coarse, known - coarse, jnp.zeros((STATS - 4 * rows, LANES), jnp.float32)], axis=0
            ).astype(retb.dtype)
            low_copies = copies.astype(retb.dtype).reshape(n, pair, LANES)
            for d in range(n):
                retb[d, s, :pair] = low_copies[d]
                retb[d, s, pair:] = known
        for o in range(1, n):
            peer = lax.rem(me + o, n)
            copy = pltpu.make_async_remote_copy(
                src_ref=retb.at[peer, slot:slot + per], dst_ref=got.at[me, slot:slot + per],
                send_sem=own_sem.at[3], recv_sem=back_recv.at[g],
                device_id={"mem": peer}, device_id_type=MESH,
            )
            copy.start()
        for s in range(slot, slot + per):
            got[me, s] = retb[me, s]

    for g, (first, last, slot, per) in enumerate(groups):
        settle(got.at[:n - 1, slot:slot + per], back_recv.at[g])
        for f in range(first, last):
            for c in range(halves):
                b = (f - first) * halves + c
                block_in = got[b % n, slot + b // n].astype(jnp.float32)
                known = block_in[pair:pair + 2 * rows] + block_in[pair + 2 * rows:pair + 4 * rows]
                forecast = cast[f, c]
                for r in range(rows):
                    part = slice(r * members, (r + 1) * members)
                    mean, ratio = known[r:r + 1], known[rows + r:rows + r + 1]
                    local = locs[c, part]
                    deviation = local * (block_in[part] - mean) + (1.0 - local) * (forecast[part] - mean)
                    out_ref[place(f, c, r), :] = mean + ratio * deviation

    for ref, i in ((halo, 0), (wide.at[:n - 1], 1), (sendb.at[:n - 1], 2), (retb.at[:n - 1], 3)):
        settle(ref, own_sem.at[i])


def solution(mesh):
    n, regs = mesh.shape["mem"], mesh.shape["reg"]

    def per_device(sample_stack, weights, offspring, localize):
        members, fields, rows, width = sample_stack.shape
        halves = width // LANES
        groups, slots = field_groups(fields, halves, n)
        count = len(groups)
        pair = rows * members
        x = sample_stack.reshape(members, fields, rows, halves, LANES).transpose(0, 1, 3, 2, 4)
        x = x.reshape(members * fields * halves * rows, LANES)
        hbm = pl.BlockSpec(memory_space=pltpu.HBM)
        vmem = pltpu.VMEM
        sem = pltpu.SemaphoreType.DMA
        f32, b16 = jnp.float32, jnp.bfloat16
        out = pl.pallas_call(
            functools.partial(kernel, n, regs, groups, fields, rows, halves, members),
            out_shape=jax.ShapeDtypeStruct(x.shape, f32),
            in_specs=[hbm] * 4,
            out_specs=pl.BlockSpec(memory_space=vmem),
            scratch_shapes=[
                vmem(x.shape, f32),
                vmem(weights.shape, f32),
                vmem(offspring.shape, jnp.int32),
                vmem(localize.shape, f32),
                vmem((fields, halves, pair, LANES), b16),
                vmem((2, fields, halves, pair, LANES), b16),
                vmem((fields, halves, pair, LANES), f32),
                vmem((n, slots, pair, LANES), b16),
                vmem((n, slots, pair, LANES), b16),
                vmem((n, slots, pair + STATS, LANES), b16),
                vmem((n, slots, pair + STATS, LANES), b16),
                vmem((n, members, LANES), f32),
                vmem((halves, pair, LANES), f32),
                vmem((n * pair, n * pair), b16),
                sem((4,)), sem((count,)), sem((count,)), sem((count,)), sem,
                pltpu.SemaphoreType.REGULAR,
            ],
            compiler_params=pltpu.CompilerParams(
                collective_id=0, has_side_effects=True, vmem_limit_bytes=32 << 20
            ),
        )(*(pltpu.with_memory_space_constraint(a, pltpu.HBM) for a in (x, weights, offspring, localize)))
        out = out.reshape(members, fields, halves, rows, LANES).transpose(0, 1, 3, 2, 4)
        return out.reshape(members, fields, rows, width)

    in_specs = (P("mem", None, "reg", None), P("reg", "mem"), P("reg", None), P("reg", None))
    return jax.shard_map(
        per_device, mesh=mesh, in_specs=in_specs, out_specs=P("mem", None, "reg", None), check_vma=False
    )
```

```python
import functools

import jax
import jax.numpy as jnp
from jax import lax
from jax.experimental import pallas as pl
from jax.experimental.pallas import tpu as pltpu
from jax.sharding import PartitionSpec as P

MESH = pl.DeviceIdType.MESH
wave_gain = 0.25
advect_gain = 0.1
diffuse_gain = 0.1
small_eps = 1e-05
LANES = 128
FLOWS = 3
STATS = 16


def field_groups(fields, sizes=(4, 4)):
    groups, first = [], 0
    for size in sizes + (fields,):
        last = min(fields, first + size)
        if last > first:
            groups.append((first, last))
        first = last
    return groups


def settle(ref, semaphore):
    pltpu.make_async_copy(ref, ref, semaphore).wait()


def sideways(block):
    width = block.shape[-1]
    return pltpu.roll(block, width - 1, 1), pltpu.roll(block, 1, 1)


def flow_step(height, east, north, rows):
    half = 0.5 * wave_gain
    new_height, new_east, new_north = {}, {}, {}
    for r in rows:
        e_right, e_left = sideways(east[r])
        h_right, h_left = sideways(height[r])
        new_height[r] = height[r] - half * ((e_right - e_left) + (north[r + 1] - north[r - 1]))
        new_east[r] = east[r] - half * (h_right - h_left)
        new_north[r] = north[r] - half * (height[r + 1] - height[r - 1])
    return new_height, new_east, new_north


def tracer_gains(east, north, rows):
    gains = {}
    for r in rows:
        e, v = (0.5 * advect_gain) * east[r], (0.5 * advect_gain) * north[r]
        gains[r] = (diffuse_gain - e, diffuse_gain + e, diffuse_gain - v, diffuse_gain + v)
    return gains


def tracer_step(tracer, gains, rows):
    new = {}
    for r in rows:
        right, left = sideways(tracer[r])
        g_right, g_left, g_up, g_low = gains[r]
        new[r] = (
            (1.0 - 4.0 * diffuse_gain) * tracer[r]
            + (g_right * right + g_left * left)
            + (g_up * tracer[r + 1] + g_low * tracer[r - 1])
        )
    return new


def kernel(
    n, regs, groups, fields, rows, halves, members,
    x_hbm, w_hbm, off_hbm, loc_hbm, out_ref,
    xs, w_ref, off_ref, loc_ref, own, halo, cast, sendb, recv, retb, got, wide, locs, pick, kept,
    own_sem, halo_recv, to_recv, back_recv, w_recv, ready,
):
    me = lax.axis_index("mem")
    band = lax.axis_index("reg")
    stride = fields * halves * rows
    pair = rows * members
    everyone = n * members
    mine = lax.rem(me, halves)
    other = halves - 1 - mine
    sibling = me + other - mine

    loads = []
    for i, (src, dst) in enumerate(((x_hbm, xs), (w_hbm, w_ref), (off_hbm, off_ref), (loc_hbm, loc_ref))):
        copy = pltpu.make_async_copy(src, dst, own_sem.at[i])
        copy.start()
        loads.append(copy)

    edge = lax.rem(band + regs - 1, regs) // (regs - 1)
    ways = ((lax.rem(band + 1, regs), 0), (lax.rem(band + regs - 1, regs), 1))
    last_band = band // (regs - 1)
    relayed = last_band + lax.rem(band + regs - 2, regs) // (regs - 1)
    relays = lax.rem(band + 1, regs) // (regs - 1) + edge
    barrier = pltpu.get_barrier_semaphore()
    for target, _ in ways:
        pl.semaphore_signal(barrier, inc=1, device_id={"reg": target}, device_id_type=MESH)
    for o in range(1, n):
        pl.semaphore_signal(
            barrier, inc=1, device_id={"mem": lax.rem(me + o, n), "reg": band - relayed}, device_id_type=MESH
        )

    def place(f, c, r):
        return pl.ds((f * halves + c) * rows + r, members, stride=stride)

    loads[0].wait()
    for f in range(fields):
        for c in range(halves):
            own[f, c] = jnp.concatenate([xs[place(f, c, r), :] for r in range(rows)], axis=0).astype(own.dtype)
    pl.semaphore_wait(barrier, 2 + (n - 1) * (1 - relayed + relays))

    @pl.when(relays == 1)
    def _():
        pl.semaphore_signal(ready, inc=1, device_id={"reg": lax.rem(band + 1, regs)}, device_id_type=MESH)

    for turn, (target, way) in enumerate(ways):
        if turn == 1:
            @pl.when(last_band == 1)
            def _():
                settle(own, own_sem.at[0])

        for g, (first, last) in enumerate(groups):
            copy = pltpu.make_async_remote_copy(
                src_ref=own.at[first:last], dst_ref=halo.at[way, first:last],
                send_sem=own_sem.at[4 * turn], recv_sem=halo_recv.at[g],
                device_id={"reg": target}, device_id_type=MESH,
            )
            copy.start()

    loads[2].wait()
    block = n * pair
    j_row = lax.broadcasted_iota(jnp.int32, (block, everyone), 0)
    wanted = (j_row // pair) * members + lax.rem(j_row, members)
    chosen = lax.broadcasted_iota(jnp.int32, (block, everyone), 1) == wanted
    source = jnp.sum(
        jnp.where(chosen, jnp.broadcast_to(off_ref[...].astype(jnp.float32), (block, everyone)), 0.0),
        axis=1, keepdims=True,
    ).astype(jnp.int32)
    row = lax.broadcasted_iota(jnp.int32, (block, 1), 0)
    target_row = (source // members) * pair + lax.rem(row // members, rows) * members + lax.rem(source, members)
    k_col = lax.broadcasted_iota(jnp.int32, (block, block), 1)
    pick[...] = (k_col == jnp.broadcast_to(target_row, (block, block))).astype(jnp.float32).astype(pick.dtype)

    loads[3].wait()
    for c in range(halves):
        locs[c] = jnp.concatenate(
            [
                jnp.broadcast_to(loc_ref[r:r + 1, c * LANES:(c + 1) * LANES], (members, LANES))
                for r in range(rows)
            ],
            axis=0,
        )
    @pl.when(relayed == 1)
    def _():
        pl.semaphore_wait(ready, 1)

    loads[1].wait()
    eye = lax.broadcasted_iota(jnp.int32, (members, members), 0) == lax.broadcasted_iota(
        jnp.int32, (members, members), 1
    )
    column = jnp.sum(jnp.where(eye, jnp.broadcast_to(w_ref[...], (members, members)), 0.0), axis=1, keepdims=True)
    wide[me] = jnp.broadcast_to(column, (members, LANES))
    for o in range(1, n):
        copy = pltpu.make_async_remote_copy(
            src_ref=wide.at[me], dst_ref=wide.at[me], send_sem=own_sem.at[1], recv_sem=w_recv,
            device_id={"mem": lax.rem(me + o, n)}, device_id_type=MESH,
        )
        copy.start()

    inner, outer = range(rows), range(-1, rows + 1)
    gains = []
    for g, (first, last) in enumerate(groups):
        settle(halo.at[:, first:last], halo_recv.at[g])

        def column_of(f):
            values = {}
            for way, base in ((0, -rows), (1, rows)):
                both = [halo[way, f, c].astype(jnp.float32) for c in range(halves)]
                for r in range(rows):
                    values[base + r] = jnp.concatenate([b[r * members:(r + 1) * members] for b in both], axis=1)
            for r in range(rows):
                values[r] = jnp.concatenate([xs[place(f, c, r), :] for c in range(halves)], axis=1)
            return values

        done = {}
        if g == 0:
            height, east, north = (column_of(f) for f in range(FLOWS))
            gains.append(tracer_gains(east, north, outer))
            flow = flow_step(height, east, north, outer)
            gains.append(tracer_gains(flow[1], flow[2], inner))
            for f, value in enumerate(flow_step(*flow, inner)):
                done[f] = value
        for f in range(max(first, FLOWS), last):
            done[f] = tracer_step(tracer_step(column_of(f), gains[0], outer), gains[1], inner)
        for f in range(first, last):
            for c in range(halves):
                both = jnp.concatenate([done[f][r][:, c * LANES:(c + 1) * LANES] for r in inner], axis=0)
                cast[f, c] = both
                sendb[c, f] = both.astype(sendb.dtype)
        for o in range(1, n):
            peer = lax.rem(me + o, n)
            copy = pltpu.make_async_remote_copy(
                src_ref=sendb.at[lax.rem(peer, halves), first:last], dst_ref=recv.at[me, first:last],
                send_sem=own_sem.at[2], recv_sem=to_recv.at[g],
                device_id={"mem": peer}, device_id_type=MESH,
            )
            copy.start()
        recv[me, first:last] = sendb[mine, first:last]

    settle(wide.at[:n - 1], w_recv)
    weight = wide[...].reshape(n, 1, members, LANES)
    inverse = 1.0 / jnp.sum(jnp.sum(weight, axis=0), axis=1, keepdims=True)

    def posterior(copies, mean, ratio, local, forecast):
        return mean + ratio * (local * (copies - mean) + (1.0 - local) * (forecast - mean))

    local = locs[mine].reshape(1, rows, members, LANES)
    for g, (first, last) in enumerate(groups):
        settle(recv.at[:n - 1, first:last], to_recv.at[g])
        for f in range(first, last):
            low_bits = recv[:, f].reshape(block, LANES)
            copies = lax.dot_general(
                pick[...], low_bits, (((1,), (0,)), ((), ())), preferred_element_type=jnp.float32
            )
            value = low_bits.astype(jnp.float32).reshape(n, rows, members, LANES)
            mean = jnp.sum(jnp.sum(weight * value, axis=0), axis=1, keepdims=True) * inverse
            departure = value - mean[None]
            variance = jnp.sum(jnp.sum(weight * departure * departure, axis=0), axis=1, keepdims=True) * inverse
            drawn = copies.reshape(n, rows, members, LANES)
            deviation = local * (drawn - mean[None]) + (1.0 - local) * departure
            spread = jnp.sum(jnp.sum(deviation * deviation, axis=0), axis=1, keepdims=True) / everyone
            ratio = jnp.sqrt((variance + small_eps) / (spread + small_eps))
            known = jnp.concatenate([mean[r] for r in range(rows)] + [ratio[r] for r in range(rows)], axis=0)
            coarse = known.astype(jnp.bfloat16).astype(jnp.float32)
            both = jnp.concatenate(
                [coarse, known - coarse, jnp.zeros((STATS - 4 * rows, LANES), jnp.float32)], axis=0
            ).astype(retb.dtype)
            kept[...] = copies.reshape(n, pair, LANES)
            retb[f, :pair] = kept[sibling].astype(retb.dtype)
            retb[f, pair:] = both
            wanted_here = kept[me]
            forecast = cast[f, mine]
            for r in range(rows):
                part = slice(r * members, (r + 1) * members)
                out_ref[place(f, mine, r), :] = posterior(
                    wanted_here[part], mean[r], ratio[r], locs[mine, part], forecast[part]
                )
        copy = pltpu.make_async_remote_copy(
            src_ref=retb.at[first:last], dst_ref=got.at[first:last],
            send_sem=own_sem.at[3], recv_sem=back_recv.at[g],
            device_id={"mem": sibling}, device_id_type=MESH,
        )
        copy.start()

    for g, (first, last) in enumerate(groups):
        settle(got.at[first:last], back_recv.at[g])
        for f in range(first, last):
            block_in = got[f].astype(jnp.float32)
            known = block_in[pair:pair + 2 * rows] + block_in[pair + 2 * rows:pair + 4 * rows]
            forecast = cast[f, other]
            for r in range(rows):
                part = slice(r * members, (r + 1) * members)
                out_ref[place(f, other, r), :] = posterior(
                    block_in[part], known[r:r + 1], known[rows + r:rows + r + 1], locs[other, part], forecast[part]
                )

    @pl.when(last_band == 0)
    def _():
        settle(own, own_sem.at[0])

    for ref, i in ((own, 4), (wide.at[:n - 1], 1), (recv.at[:n - 1], 2), (retb, 3)):
        settle(ref, own_sem.at[i])


def solution(mesh):
    n, regs = mesh.shape["mem"], mesh.shape["reg"]

    def per_device(sample_stack, weights, offspring, localize):
        members, fields, rows, width = sample_stack.shape
        halves = width // LANES
        groups = field_groups(fields)
        count = len(groups)
        pair = rows * members
        x = sample_stack.reshape(members, fields, rows, halves, LANES).transpose(0, 1, 3, 2, 4)
        x = x.reshape(members * fields * halves * rows, LANES)
        hbm = pl.BlockSpec(memory_space=pltpu.HBM)
        vmem = pltpu.VMEM
        sem = pltpu.SemaphoreType.DMA
        f32, b16 = jnp.float32, jnp.bfloat16
        out = pl.pallas_call(
            functools.partial(kernel, n, regs, groups, fields, rows, halves, members),
            out_shape=jax.ShapeDtypeStruct(x.shape, f32),
            in_specs=[hbm] * 4,
            out_specs=pl.BlockSpec(memory_space=vmem),
            scratch_shapes=[
                vmem(x.shape, f32),
                vmem(weights.shape, f32),
                vmem(offspring.shape, jnp.int32),
                vmem(localize.shape, f32),
                vmem((fields, halves, pair, LANES), b16),
                vmem((2, fields, halves, pair, LANES), b16),
                vmem((fields, halves, pair, LANES), f32),
                vmem((halves, fields, pair, LANES), b16),
                vmem((n, fields, pair, LANES), b16),
                vmem((fields, pair + STATS, LANES), b16),
                vmem((fields, pair + STATS, LANES), b16),
                vmem((n, members, LANES), f32),
                vmem((halves, pair, LANES), f32),
                vmem((n * pair, n * pair), b16),
                vmem((n, pair, LANES), f32),
                sem((5,)), sem((count,)), sem((count,)), sem((count,)), sem,
                pltpu.SemaphoreType.REGULAR,
            ],
            compiler_params=pltpu.CompilerParams(
                collective_id=0, has_side_effects=True, vmem_limit_bytes=32 << 20
            ),
        )(*(pltpu.with_memory_space_constraint(a, pltpu.HBM) for a in (x, weights, offspring, localize)))
        out = out.reshape(members, fields, halves, rows, LANES).transpose(0, 1, 3, 2, 4)
        return out.reshape(members, fields, rows, width)

    in_specs = (P("mem", None, "reg", None), P("reg", "mem"), P("reg", None), P("reg", None))
    return jax.shard_map(
        per_device, mesh=mesh, in_specs=in_specs, out_specs=P("mem", None, "reg", None), check_vma=False
    )
```

```python
import functools

import jax
import jax.numpy as jnp
from jax import lax
from jax.experimental import pallas as pl
from jax.experimental.pallas import tpu as pltpu
from jax.sharding import PartitionSpec as P

MESH = pl.DeviceIdType.MESH
wave_gain = 0.25
advect_gain = 0.1
diffuse_gain = 0.1
small_eps = 1e-05
LANES = 128
FLOWS = 3
STATS = 16


def field_groups(fields, sizes=(3, 4)):
    groups, first = [], 0
    for size in sizes + (fields,):
        last = min(fields, first + size)
        if last > first:
            groups.append((first, last))
        first = last
    return groups


def settle(ref, semaphore):
    pltpu.make_async_copy(ref, ref, semaphore).wait()


def sideways(block):
    width = block.shape[-1]
    return pltpu.roll(block, width - 1, 1), pltpu.roll(block, 1, 1)


def flow_step(height, east, north, rows):
    half = 0.5 * wave_gain
    new_height, new_east, new_north = {}, {}, {}
    for r in rows:
        e_right, e_left = sideways(east[r])
        h_right, h_left = sideways(height[r])
        new_height[r] = height[r] - half * ((e_right - e_left) + (north[r + 1] - north[r - 1]))
        new_east[r] = east[r] - half * (h_right - h_left)
        new_north[r] = north[r] - half * (height[r + 1] - height[r - 1])
    return new_height, new_east, new_north


def tracer_gains(east, north, rows):
    gains = {}
    for r in rows:
        e, v = (0.5 * advect_gain) * east[r], (0.5 * advect_gain) * north[r]
        gains[r] = (diffuse_gain - e, diffuse_gain + e, diffuse_gain - v, diffuse_gain + v)
    return gains


def tracer_step(tracer, gains, rows):
    new = {}
    for r in rows:
        right, left = sideways(tracer[r])
        g_right, g_left, g_up, g_low = gains[r]
        new[r] = (
            (1.0 - 4.0 * diffuse_gain) * tracer[r]
            + (g_right * right + g_left * left)
            + (g_up * tracer[r + 1] + g_low * tracer[r - 1])
        )
    return new


def kernel(
    n, regs, groups, fields, rows, halves, members,
    x_hbm, w_hbm, off_hbm, loc_hbm, out_ref,
    xs, w_ref, off_ref, loc_ref, own, halo, cast, sendb, recv, retb, got, wide, locs, pick, kept,
    own_sem, halo_recv, to_recv, back_recv, w_recv, ready, go,
):
    me = lax.axis_index("mem")
    band = lax.axis_index("reg")
    stride = fields * halves * rows
    pair = rows * members
    everyone = n * members
    mine = lax.rem(me, halves)
    other = halves - 1 - mine
    sibling = me + other - mine

    loads = []
    for i, (src, dst) in enumerate(((x_hbm, xs), (w_hbm, w_ref), (off_hbm, off_ref), (loc_hbm, loc_ref))):
        copy = pltpu.make_async_copy(src, dst, own_sem.at[i])
        copy.start()
        loads.append(copy)

    first_band = lax.rem(band + regs - 1, regs) // (regs - 1)
    second_band = lax.rem(band + regs - 2, regs) // (regs - 1)
    last_band = band // (regs - 1)
    corner = me // (n - 1)
    barrier = pltpu.get_barrier_semaphore()

    def greet(semaphore, **target):
        pl.semaphore_signal(semaphore, inc=1, device_id=target, device_id_type=MESH)

    @pl.when(corner == 0)
    def _():
        greet(barrier, mem=n - 1)

    @pl.when(last_band == 0)
    def _():
        greet(barrier, reg=band + 1)

    @pl.when(first_band + second_band == 1)
    def _():
        greet(barrier, reg=(regs - 1) * first_band)

    def place(f, c, r):
        return pl.ds((f * halves + c) * rows + r, members, stride=stride)

    pl.semaphore_wait(barrier, 1 + last_band + (n - 1) * corner)

    @pl.when(first_band + second_band == 0)
    def _():
        greet(go, reg=band - 1)

    @pl.when(last_band == 1)
    def _():
        greet(go, reg=0)

    loads[0].wait()
    for f in range(fields):
        for c in range(halves):
            own[f, c] = jnp.concatenate([xs[place(f, c, r), :] for r in range(rows)], axis=0).astype(own.dtype)

    up = first_band + last_band
    ways = (
        (lax.rem(band + 1 + (1 - up) * (regs - 2), regs), 1 - up),
        (lax.rem(band + 1 + up * (regs - 2), regs), up),
    )
    for turn, (target, way) in enumerate(ways):
        if turn == 1:
            @pl.when(corner == 1)
            def _():
                for d in range(n - 1):
                    greet(ready, mem=d)

            @pl.when(last_band == 1)
            def _():
                settle(own, own_sem.at[0])

            @pl.when(last_band == 0)
            def _():
                pl.semaphore_wait(go, 1)

        for g, (first, last) in enumerate(groups):
            copy = pltpu.make_async_remote_copy(
                src_ref=own.at[first:last], dst_ref=halo.at[way, first:last],
                send_sem=own_sem.at[4 * turn], recv_sem=halo_recv.at[g],
                device_id={"reg": target}, device_id_type=MESH,
            )
            copy.start()

    loads[2].wait()
    block = n * pair
    j_row = lax.broadcasted_iota(jnp.int32, (block, everyone), 0)
    wanted = (j_row // pair) * members + lax.rem(j_row, members)
    chosen = lax.broadcasted_iota(jnp.int32, (block, everyone), 1) == wanted
    source = jnp.sum(
        jnp.where(chosen, jnp.broadcast_to(off_ref[...].astype(jnp.float32), (block, everyone)), 0.0),
        axis=1, keepdims=True,
    ).astype(jnp.int32)
    row = lax.broadcasted_iota(jnp.int32, (block, 1), 0)
    target_row = (source // members) * pair + lax.rem(row // members, rows) * members + lax.rem(source, members)
    k_col = lax.broadcasted_iota(jnp.int32, (block, block), 1)
    pick[...] = (k_col == jnp.broadcast_to(target_row, (block, block))).astype(jnp.float32).astype(pick.dtype)

    loads[3].wait()
    for c in range(halves):
        locs[c] = jnp.concatenate(
            [
                jnp.broadcast_to(loc_ref[r:r + 1, c * LANES:(c + 1) * LANES], (members, LANES))
                for r in range(rows)
            ],
            axis=0,
        )
    @pl.when(corner == 0)
    def _():
        pl.semaphore_wait(ready, 1)

    loads[1].wait()
    eye = lax.broadcasted_iota(jnp.int32, (members, members), 0) == lax.broadcasted_iota(
        jnp.int32, (members, members), 1
    )
    column = jnp.sum(jnp.where(eye, jnp.broadcast_to(w_ref[...], (members, members)), 0.0), axis=1, keepdims=True)
    wide[me] = jnp.broadcast_to(column, (members, LANES))
    for o in range(1, n):
        copy = pltpu.make_async_remote_copy(
            src_ref=wide.at[me], dst_ref=wide.at[me], send_sem=own_sem.at[1], recv_sem=w_recv,
            device_id={"mem": lax.rem(me + o, n)}, device_id_type=MESH,
        )
        copy.start()

    inner, outer = range(rows), range(-1, rows + 1)
    gains = []
    for g, (first, last) in enumerate(groups):
        settle(halo.at[:, first:last], halo_recv.at[g])

        def column_of(f):
            values = {}
            for way, base in ((0, -rows), (1, rows)):
                both = [halo[way, f, c].astype(jnp.float32) for c in range(halves)]
                for r in range(rows):
                    values[base + r] = jnp.concatenate([b[r * members:(r + 1) * members] for b in both], axis=1)
            for r in range(rows):
                values[r] = jnp.concatenate([xs[place(f, c, r), :] for c in range(halves)], axis=1)
            return values

        done = {}
        if g == 0:
            height, east, north = (column_of(f) for f in range(FLOWS))
            gains.append(tracer_gains(east, north, outer))
            flow = flow_step(height, east, north, outer)
            gains.append(tracer_gains(flow[1], flow[2], inner))
            for f, value in enumerate(flow_step(*flow, inner)):
                done[f] = value
        for f in range(max(first, FLOWS), last):
            done[f] = tracer_step(tracer_step(column_of(f), gains[0], outer), gains[1], inner)
        for f in range(first, last):
            for c in range(halves):
                both = jnp.concatenate([done[f][r][:, c * LANES:(c + 1) * LANES] for r in inner], axis=0)
                cast[f, c] = both
                sendb[c, f] = both.astype(sendb.dtype)
        for o in range(1, n):
            peer = lax.rem(me + o, n)
            copy = pltpu.make_async_remote_copy(
                src_ref=sendb.at[lax.rem(peer, halves), first:last], dst_ref=recv.at[me, first:last],
                send_sem=own_sem.at[2], recv_sem=to_recv.at[g],
                device_id={"mem": peer}, device_id_type=MESH,
            )
            copy.start()
        recv[me, first:last] = sendb[mine, first:last]

    settle(wide.at[:n - 1], w_recv)
    weight = wide[...].reshape(n, 1, members, LANES)
    inverse = 1.0 / jnp.sum(jnp.sum(weight, axis=0), axis=1, keepdims=True)

    def posterior(copies, mean, ratio, local, forecast):
        return mean + ratio * (local * (copies - mean) + (1.0 - local) * (forecast - mean))

    local = locs[mine].reshape(1, rows, members, LANES)
    for g, (first, last) in enumerate(groups):
        settle(recv.at[:n - 1, first:last], to_recv.at[g])
        for f in range(first, last):
            low_bits = recv[:, f].reshape(block, LANES)
            copies = lax.dot_general(
                pick[...], low_bits, (((1,), (0,)), ((), ())), preferred_element_type=jnp.float32
            )
            value = low_bits.astype(jnp.float32).reshape(n, rows, members, LANES)
            mean = jnp.sum(jnp.sum(weight * value, axis=0), axis=1, keepdims=True) * inverse
            departure = value - mean[None]
            variance = jnp.sum(jnp.sum(weight * departure * departure, axis=0), axis=1, keepdims=True) * inverse
            drawn = copies.reshape(n, rows, members, LANES)
            deviation = local * (drawn - mean[None]) + (1.0 - local) * departure
            spread = jnp.sum(jnp.sum(deviation * deviation, axis=0), axis=1, keepdims=True) / everyone
            ratio = jnp.sqrt((variance + small_eps) / (spread + small_eps))
            known = jnp.concatenate([mean[r] for r in range(rows)] + [ratio[r] for r in range(rows)], axis=0)
            coarse = known.astype(jnp.bfloat16).astype(jnp.float32)
            both = jnp.concatenate(
                [coarse, known - coarse, jnp.zeros((STATS - 4 * rows, LANES), jnp.float32)], axis=0
            ).astype(retb.dtype)
            kept[...] = copies.reshape(n, pair, LANES)
            retb[f, :pair] = kept[sibling].astype(retb.dtype)
            retb[f, pair:] = both
            wanted_here = kept[me]
            forecast = cast[f, mine]
            for r in range(rows):
                part = slice(r * members, (r + 1) * members)
                out_ref[place(f, mine, r), :] = posterior(
                    wanted_here[part], mean[r], ratio[r], locs[mine, part], forecast[part]
                )
        copy = pltpu.make_async_remote_copy(
            src_ref=retb.at[first:last], dst_ref=got.at[first:last],
            send_sem=own_sem.at[3], recv_sem=back_recv.at[g],
            device_id={"mem": sibling}, device_id_type=MESH,
        )
        copy.start()

    for g, (first, last) in enumerate(groups):
        settle(got.at[first:last], back_recv.at[g])
        for f in range(first, last):
            block_in = got[f].astype(jnp.float32)
            known = block_in[pair:pair + 2 * rows] + block_in[pair + 2 * rows:pair + 4 * rows]
            forecast = cast[f, other]
            for r in range(rows):
                part = slice(r * members, (r + 1) * members)
                out_ref[place(f, other, r), :] = posterior(
                    block_in[part], known[r:r + 1], known[rows + r:rows + r + 1], locs[other, part], forecast[part]
                )

    @pl.when(last_band == 0)
    def _():
        settle(own, own_sem.at[0])

    for ref, i in ((own, 4), (wide.at[:n - 1], 1), (recv.at[:n - 1], 2), (retb, 3)):
        settle(ref, own_sem.at[i])


def solution(mesh):
    n, regs = mesh.shape["mem"], mesh.shape["reg"]

    def per_device(sample_stack, weights, offspring, localize):
        members, fields, rows, width = sample_stack.shape
        halves = width // LANES
        groups = field_groups(fields)
        count = len(groups)
        pair = rows * members
        x = sample_stack.reshape(members, fields, rows, halves, LANES).transpose(0, 1, 3, 2, 4)
        x = x.reshape(members * fields * halves * rows, LANES)
        hbm = pl.BlockSpec(memory_space=pltpu.HBM)
        vmem = pltpu.VMEM
        sem = pltpu.SemaphoreType.DMA
        f32, b16 = jnp.float32, jnp.bfloat16
        out = pl.pallas_call(
            functools.partial(kernel, n, regs, groups, fields, rows, halves, members),
            out_shape=jax.ShapeDtypeStruct(x.shape, f32),
            in_specs=[hbm] * 4,
            out_specs=pl.BlockSpec(memory_space=vmem),
            scratch_shapes=[
                vmem(x.shape, f32),
                vmem(weights.shape, f32),
                vmem(offspring.shape, jnp.int32),
                vmem(localize.shape, f32),
                vmem((fields, halves, pair, LANES), b16),
                vmem((2, fields, halves, pair, LANES), b16),
                vmem((fields, halves, pair, LANES), f32),
                vmem((halves, fields, pair, LANES), b16),
                vmem((n, fields, pair, LANES), b16),
                vmem((fields, pair + STATS, LANES), b16),
                vmem((fields, pair + STATS, LANES), b16),
                vmem((n, members, LANES), f32),
                vmem((halves, pair, LANES), f32),
                vmem((n * pair, n * pair), b16),
                vmem((n, pair, LANES), f32),
                sem((5,)), sem((count,)), sem((count,)), sem((count,)), sem,
                pltpu.SemaphoreType.REGULAR, pltpu.SemaphoreType.REGULAR,
            ],
            compiler_params=pltpu.CompilerParams(
                collective_id=0, has_side_effects=True, vmem_limit_bytes=32 << 20
            ),
        )(*(pltpu.with_memory_space_constraint(a, pltpu.HBM) for a in (x, weights, offspring, localize)))
        out = out.reshape(members, fields, halves, rows, LANES).transpose(0, 1, 3, 2, 4)
        return out.reshape(members, fields, rows, width)

    in_specs = (P("mem", None, "reg", None), P("reg", "mem"), P("reg", None), P("reg", None))
    return jax.shard_map(
        per_device, mesh=mesh, in_specs=in_specs, out_specs=P("mem", None, "reg", None), check_vma=False
    )
```

```python
import functools

import jax
import jax.numpy as jnp
from jax import lax
from jax.experimental import pallas as pl
from jax.experimental.pallas import tpu as pltpu
from jax.sharding import PartitionSpec as P

MESH = pl.DeviceIdType.MESH
wave_gain = 0.25
advect_gain = 0.1
diffuse_gain = 0.1
small_eps = 1e-05
LANES = 128
FLOWS = 3
STATS = 16


def field_groups(fields, sizes=(3, 4, 3)):
    groups, first = [], 0
    for size in sizes + (fields,):
        last = min(fields, first + size)
        if last > first:
            groups.append((first, last))
        first = last
    return groups


def settle(ref, semaphore):
    pltpu.make_async_copy(ref, ref, semaphore).wait()


def sideways(block):
    width = block.shape[-1]
    return pltpu.roll(block, width - 1, 1), pltpu.roll(block, 1, 1)


def flow_step(height, east, north, rows):
    half = 0.5 * wave_gain
    new_height, new_east, new_north = {}, {}, {}
    for r in rows:
        e_right, e_left = sideways(east[r])
        h_right, h_left = sideways(height[r])
        new_height[r] = height[r] - half * ((e_right - e_left) + (north[r + 1] - north[r - 1]))
        new_east[r] = east[r] - half * (h_right - h_left)
        new_north[r] = north[r] - half * (height[r + 1] - height[r - 1])
    return new_height, new_east, new_north


def tracer_gains(east, north, rows):
    gains = {}
    for r in rows:
        e, v = (0.5 * advect_gain) * east[r], (0.5 * advect_gain) * north[r]
        gains[r] = (diffuse_gain - e, diffuse_gain + e, diffuse_gain - v, diffuse_gain + v)
    return gains


def tracer_step(tracer, gains, rows):
    new = {}
    for r in rows:
        right, left = sideways(tracer[r])
        g_right, g_left, g_up, g_low = gains[r]
        new[r] = (
            (1.0 - 4.0 * diffuse_gain) * tracer[r]
            + (g_right * right + g_left * left)
            + (g_up * tracer[r + 1] + g_low * tracer[r - 1])
        )
    return new


def kernel(
    n, regs, groups, fields, rows, halves, members,
    x_hbm, w_hbm, off_hbm, loc_hbm, out_ref,
    xs, w_ref, off_ref, loc_ref, own, halo, cast, sendb, recv, retb, got, wide, locs, pick, kept,
    own_sem, halo_recv, to_recv, back_recv, w_recv, ready, go,
):
    me = lax.axis_index("mem")
    band = lax.axis_index("reg")
    stride = fields * halves * rows
    pair = rows * members
    everyone = n * members
    mine = lax.rem(me, halves)
    other = halves - 1 - mine
    sibling = me + other - mine

    loads = [
        pltpu.make_async_copy(src, dst, own_sem.at[i])
        for i, (src, dst) in enumerate(((x_hbm, xs), (w_hbm, w_ref), (off_hbm, off_ref), (loc_hbm, loc_ref)))
    ]
    loads[0].start()

    first_band = lax.rem(band + regs - 1, regs) // (regs - 1)
    second_band = lax.rem(band + regs - 2, regs) // (regs - 1)
    last_band = band // (regs - 1)
    corner = me // (n - 1)
    barrier = pltpu.get_barrier_semaphore()

    def greet(semaphore, **target):
        pl.semaphore_signal(semaphore, inc=1, device_id=target, device_id_type=MESH)

    @pl.when(corner == 0)
    def _():
        greet(barrier, mem=n - 1)

    @pl.when(last_band == 0)
    def _():
        greet(barrier, reg=band + 1)

    @pl.when(first_band + second_band == 1)
    def _():
        greet(barrier, reg=(regs - 1) * first_band)

    def place(f, c, r):
        return pl.ds((f * halves + c) * rows + r, members, stride=stride)

    pl.semaphore_wait(barrier, 1 + last_band + (n - 1) * corner)

    @pl.when(first_band + second_band == 0)
    def _():
        greet(go, reg=band - 1)

    @pl.when(last_band == 1)
    def _():
        greet(go, reg=0)

    loads[0].wait()
    up = first_band + last_band
    ways = (
        (lax.rem(band + 1 + (1 - up) * (regs - 2), regs), 1 - up),
        (lax.rem(band + 1 + up * (regs - 2), regs), up),
    )
    for turn, (target, way) in enumerate(ways):
        if turn == 1:
            for load in loads[1:]:
                load.start()

            @pl.when(corner == 1)
            def _():
                for d in range(n - 1):
                    greet(ready, mem=d)

            @pl.when(last_band == 1)
            def _():
                settle(own, own_sem.at[0])

            @pl.when(last_band == 0)
            def _():
                pl.semaphore_wait(go, 1)

        for g, (first, last) in enumerate(groups):
            if turn == 0:
                for f in range(first, last):
                    for c in range(halves):
                        rounded = jnp.concatenate([xs[place(f, c, r), :] for r in range(rows)], axis=0)
                        own[f, c] = rounded.astype(own.dtype)
            copy = pltpu.make_async_remote_copy(
                src_ref=own.at[first:last], dst_ref=halo.at[way, first:last],
                send_sem=own_sem.at[4 * turn], recv_sem=halo_recv.at[g],
                device_id={"reg": target}, device_id_type=MESH,
            )
            copy.start()

    loads[2].wait()
    block = n * pair
    j_row = lax.broadcasted_iota(jnp.int32, (block, everyone), 0)
    wanted = (j_row // pair) * members + lax.rem(j_row, members)
    chosen = lax.broadcasted_iota(jnp.int32, (block, everyone), 1) == wanted
    source = jnp.sum(
        jnp.where(chosen, jnp.broadcast_to(off_ref[...].astype(jnp.float32), (block, everyone)), 0.0),
        axis=1, keepdims=True,
    ).astype(jnp.int32)
    row = lax.broadcasted_iota(jnp.int32, (block, 1), 0)
    target_row = (source // members) * pair + lax.rem(row // members, rows) * members + lax.rem(source, members)
    k_col = lax.broadcasted_iota(jnp.int32, (block, block), 1)
    pick[...] = (k_col == jnp.broadcast_to(target_row, (block, block))).astype(jnp.float32).astype(pick.dtype)

    loads[3].wait()
    for c in range(halves):
        locs[c] = jnp.concatenate(
            [
                jnp.broadcast_to(loc_ref[r:r + 1, c * LANES:(c + 1) * LANES], (members, LANES))
                for r in range(rows)
            ],
            axis=0,
        )
    @pl.when(corner == 0)
    def _():
        pl.semaphore_wait(ready, 1)

    loads[1].wait()
    eye = lax.broadcasted_iota(jnp.int32, (members, members), 0) == lax.broadcasted_iota(
        jnp.int32, (members, members), 1
    )
    column = jnp.sum(jnp.where(eye, jnp.broadcast_to(w_ref[...], (members, members)), 0.0), axis=1, keepdims=True)
    wide[me] = jnp.broadcast_to(column, (members, LANES))
    for o in range(1, n):
        copy = pltpu.make_async_remote_copy(
            src_ref=wide.at[me], dst_ref=wide.at[me], send_sem=own_sem.at[1], recv_sem=w_recv,
            device_id={"mem": lax.rem(me + o, n)}, device_id_type=MESH,
        )
        copy.start()

    half = n // 2
    place_of_me = me * (1 - me // half) + (me // half) * (half + lax.rem(me + half - 2, half))

    def send(g, turns):
        first, last = groups[g]
        for d in turns:
            slot = d + (d - place_of_me + n) // n
            upper = slot // half
            peer = slot * (1 - upper) + upper * (half + lax.rem(slot + 2, half))
            copy = pltpu.make_async_remote_copy(
                src_ref=sendb.at[lax.rem(peer, halves), first:last], dst_ref=recv.at[me, first:last],
                send_sem=own_sem.at[2], recv_sem=to_recv.at[g],
                device_id={"mem": peer}, device_id_type=MESH,
            )
            copy.start()

    inner, outer = range(rows), range(-1, rows + 1)
    gains = []
    for g, (first, last) in enumerate(groups):
        settle(halo.at[:, first:last], halo_recv.at[g])

        def column_of(f):
            values = {}
            for way, base in ((0, -rows), (1, rows)):
                both = [halo[way, f, c].astype(jnp.float32) for c in range(halves)]
                for r in range(rows):
                    values[base + r] = jnp.concatenate([b[r * members:(r + 1) * members] for b in both], axis=1)
            for r in range(rows):
                values[r] = jnp.concatenate([xs[place(f, c, r), :] for c in range(halves)], axis=1)
            return values

        done = {}
        if g == 0:
            height, east, north = (column_of(f) for f in range(FLOWS))
            gains.append(tracer_gains(east, north, outer))
            flow = flow_step(height, east, north, outer)
            gains.append(tracer_gains(flow[1], flow[2], inner))
            for f, value in enumerate(flow_step(*flow, inner)):
                done[f] = value
        for f in range(max(first, FLOWS), last):
            done[f] = tracer_step(tracer_step(column_of(f), gains[0], outer), gains[1], inner)
        for f in range(first, last):
            for c in range(halves):
                both = jnp.concatenate([done[f][r][:, c * LANES:(c + 1) * LANES] for r in inner], axis=0)
                cast[f, c] = both
                sendb[c, f] = both.astype(sendb.dtype)
        send(g, range(n - 3))
        recv[me, first:last] = sendb[mine, first:last]
    for g in range(len(groups)):
        send(g, range(n - 3, n - 1))

    settle(wide.at[:n - 1], w_recv)
    weight = wide[...].reshape(n, 1, members, LANES)
    inverse = 1.0 / jnp.sum(jnp.sum(weight, axis=0), axis=1, keepdims=True)

    def posterior(copies, mean, ratio, local, forecast):
        return mean + ratio * (local * (copies - mean) + (1.0 - local) * (forecast - mean))

    local = locs[mine].reshape(1, rows, members, LANES)
    for g, (first, last) in enumerate(groups):
        settle(recv.at[:n - 1, first:last], to_recv.at[g])
        summary = {}
        for f in range(first, last):
            low_bits = recv[:, f].reshape(block, LANES)
            copies = lax.dot_general(
                pick[...], low_bits, (((1,), (0,)), ((), ())), preferred_element_type=jnp.float32
            )
            value = low_bits.astype(jnp.float32).reshape(n, rows, members, LANES)
            mean = jnp.sum(jnp.sum(weight * value, axis=0), axis=1, keepdims=True) * inverse
            departure = value - mean[None]
            variance = jnp.sum(jnp.sum(weight * departure * departure, axis=0), axis=1, keepdims=True) * inverse
            drawn = copies.reshape(n, rows, members, LANES)
            deviation = local * (drawn - mean[None]) + (1.0 - local) * departure
            spread = jnp.sum(jnp.sum(deviation * deviation, axis=0), axis=1, keepdims=True) / everyone
            ratio = jnp.sqrt((variance + small_eps) / (spread + small_eps))
            known = jnp.concatenate([mean[r] for r in range(rows)] + [ratio[r] for r in range(rows)], axis=0)
            coarse = known.astype(jnp.bfloat16).astype(jnp.float32)
            both = jnp.concatenate(
                [coarse, known - coarse, jnp.zeros((STATS - 4 * rows, LANES), jnp.float32)], axis=0
            ).astype(retb.dtype)
            kept[f] = copies.reshape(n, pair, LANES)
            retb[f, :pair] = kept[f, sibling].astype(retb.dtype)
            retb[f, pair:] = both
            summary[f] = mean, ratio
        copy = pltpu.make_async_remote_copy(
            src_ref=retb.at[first:last], dst_ref=got.at[first:last],
            send_sem=own_sem.at[3], recv_sem=back_recv.at[g],
            device_id={"mem": sibling}, device_id_type=MESH,
        )
        copy.start()
        for f in range(first, last):
            mean, ratio = summary[f]
            wanted_here = kept[f, me]
            forecast = cast[f, mine]
            for r in range(rows):
                part = slice(r * members, (r + 1) * members)
                out_ref[place(f, mine, r), :] = posterior(
                    wanted_here[part], mean[r], ratio[r], locs[mine, part], forecast[part]
                )

    for g, (first, last) in enumerate(groups):
        settle(got.at[first:last], back_recv.at[g])
        for f in range(first, last):
            block_in = got[f].astype(jnp.float32)
            known = block_in[pair:pair + 2 * rows] + block_in[pair + 2 * rows:pair + 4 * rows]
            forecast = cast[f, other]
            for r in range(rows):
                part = slice(r * members, (r + 1) * members)
                out_ref[place(f, other, r), :] = posterior(
                    block_in[part], known[r:r + 1], known[rows + r:rows + r + 1], locs[other, part], forecast[part]
                )

    @pl.when(last_band == 0)
    def _():
        settle(own, own_sem.at[0])

    for ref, i in ((own, 4), (wide.at[:n - 1], 1), (recv.at[:n - 1], 2), (retb, 3)):
        settle(ref, own_sem.at[i])


def solution(mesh):
    n, regs = mesh.shape["mem"], mesh.shape["reg"]

    def per_device(sample_stack, weights, offspring, localize):
        members, fields, rows, width = sample_stack.shape
        halves = width // LANES
        groups = field_groups(fields)
        count = len(groups)
        pair = rows * members
        x = sample_stack.reshape(members, fields, rows, halves, LANES).transpose(0, 1, 3, 2, 4)
        x = x.reshape(members * fields * halves * rows, LANES)
        hbm = pl.BlockSpec(memory_space=pltpu.HBM)
        vmem = pltpu.VMEM
        sem = pltpu.SemaphoreType.DMA
        f32, b16 = jnp.float32, jnp.bfloat16
        out = pl.pallas_call(
            functools.partial(kernel, n, regs, groups, fields, rows, halves, members),
            out_shape=jax.ShapeDtypeStruct(x.shape, f32),
            in_specs=[hbm] * 4,
            out_specs=pl.BlockSpec(memory_space=vmem),
            scratch_shapes=[
                vmem(x.shape, f32),
                vmem(weights.shape, f32),
                vmem(offspring.shape, jnp.int32),
                vmem(localize.shape, f32),
                vmem((fields, halves, pair, LANES), b16),
                vmem((2, fields, halves, pair, LANES), b16),
                vmem((fields, halves, pair, LANES), f32),
                vmem((halves, fields, pair, LANES), b16),
                vmem((n, fields, pair, LANES), b16),
                vmem((fields, pair + STATS, LANES), b16),
                vmem((fields, pair + STATS, LANES), b16),
                vmem((n, members, LANES), f32),
                vmem((halves, pair, LANES), f32),
                vmem((n * pair, n * pair), b16),
                vmem((fields, n, pair, LANES), f32),
                sem((5,)), sem((count,)), sem((count,)), sem((count,)), sem,
                pltpu.SemaphoreType.REGULAR, pltpu.SemaphoreType.REGULAR,
            ],
            compiler_params=pltpu.CompilerParams(
                collective_id=0, has_side_effects=True, vmem_limit_bytes=32 << 20
            ),
        )(*(pltpu.with_memory_space_constraint(a, pltpu.HBM) for a in (x, weights, offspring, localize)))
        out = out.reshape(members, fields, halves, rows, LANES).transpose(0, 1, 3, 2, 4)
        return out.reshape(members, fields, rows, width)

    in_specs = (P("mem", None, "reg", None), P("reg", "mem"), P("reg", None), P("reg", None))
    return jax.shard_map(
        per_device, mesh=mesh, in_specs=in_specs, out_specs=P("mem", None, "reg", None), check_vma=False
    )
```

```python
import functools

import jax
import jax.numpy as jnp
from jax import lax
from jax.experimental import pallas as pl
from jax.experimental.pallas import tpu as pltpu
from jax.sharding import PartitionSpec as P

MESH = pl.DeviceIdType.MESH
wave_gain = 0.25
advect_gain = 0.1
diffuse_gain = 0.1
small_eps = 1e-05
LANES = 128
FLOWS = 3
STATS = 16


def field_groups(fields, sizes=(4, 4)):
    groups, first = [], 0
    for size in sizes + (fields,):
        last = min(fields, first + size)
        if last > first:
            groups.append((first, last))
        first = last
    return groups


def settle(ref, semaphore):
    pltpu.make_async_copy(ref, ref, semaphore).wait()


def sideways(block):
    width = block.shape[-1]
    return pltpu.roll(block, width - 1, 1), pltpu.roll(block, 1, 1)


def flow_step(height, east, north, rows):
    half = 0.5 * wave_gain
    new_height, new_east, new_north = {}, {}, {}
    for r in rows:
        e_right, e_left = sideways(east[r])
        h_right, h_left = sideways(height[r])
        new_height[r] = height[r] - half * ((e_right - e_left) + (north[r + 1] - north[r - 1]))
        new_east[r] = east[r] - half * (h_right - h_left)
        new_north[r] = north[r] - half * (height[r + 1] - height[r - 1])
    return new_height, new_east, new_north


def tracer_gains(east, north, rows):
    gains = {}
    for r in rows:
        e, v = (0.5 * advect_gain) * east[r], (0.5 * advect_gain) * north[r]
        gains[r] = (diffuse_gain - e, diffuse_gain + e, diffuse_gain - v, diffuse_gain + v)
    return gains


def tracer_step(tracer, gains, rows):
    new = {}
    for r in rows:
        right, left = sideways(tracer[r])
        g_right, g_left, g_up, g_low = gains[r]
        new[r] = (
            (1.0 - 4.0 * diffuse_gain) * tracer[r]
            + (g_right * right + g_left * left)
            + (g_up * tracer[r + 1] + g_low * tracer[r - 1])
        )
    return new


def kernel(
    n, regs, groups, fields, rows, halves, members,
    x_hbm, w_hbm, off_hbm, loc_hbm, out_ref,
    xs, w_ref, off_ref, loc_ref, own, halo, cast, sendb, recv, retb, got, wide, locs, pick, kept,
    own_sem, halo_recv, to_recv, w_recv, ready, go,
):
    me = lax.axis_index("mem")
    band = lax.axis_index("reg")
    stride = fields * halves * rows
    pair = rows * members
    everyone = n * members
    mine = lax.rem(me, halves)
    other = halves - 1 - mine
    sibling = me + other - mine

    loads = [
        pltpu.make_async_copy(src, dst, own_sem.at[i])
        for i, (src, dst) in enumerate(((x_hbm, xs), (w_hbm, w_ref), (off_hbm, off_ref), (loc_hbm, loc_ref)))
    ]
    loads[0].start()

    first_band = lax.rem(band + regs - 1, regs) // (regs - 1)
    second_band = lax.rem(band + regs - 2, regs) // (regs - 1)
    last_band = band // (regs - 1)
    corner = lax.rem(me + 1, n) // (n - 1)
    barrier = pltpu.get_barrier_semaphore()

    def greet(semaphore, **target):
        pl.semaphore_signal(semaphore, inc=1, device_id=target, device_id_type=MESH)

    @pl.when(corner == 0)
    def _():
        greet(barrier, mem=n - 2)

    @pl.when(last_band == 0)
    def _():
        greet(barrier, reg=band + 1)

    @pl.when(first_band + second_band == 1)
    def _():
        greet(barrier, reg=(regs - 1) * first_band)

    def place(f, c, r):
        return pl.ds((f * halves + c) * rows + r, members, stride=stride)

    pl.semaphore_wait(barrier, 1 + last_band + (n - 1) * corner)

    @pl.when(first_band + second_band == 0)
    def _():
        greet(go, reg=band - 1)

    @pl.when(last_band == 1)
    def _():
        greet(go, reg=0)

    loads[0].wait()
    up = first_band + last_band
    ways = (
        (lax.rem(band + 1 + (1 - up) * (regs - 2), regs), 1 - up),
        (lax.rem(band + 1 + up * (regs - 2), regs), up),
    )
    for turn, (target, way) in enumerate(ways):
        if turn == 1:
            for load in loads[1:]:
                load.start()

            @pl.when(corner == 1)
            def _():
                for d in (*range(n - 2), n - 1):
                    greet(ready, mem=d)

            @pl.when(last_band == 1)
            def _():
                settle(own, own_sem.at[0])

            @pl.when(last_band == 0)
            def _():
                pl.semaphore_wait(go, 1)

        for g, (first, last) in enumerate(groups):
            if turn == 0:
                for f in range(first, last):
                    for c in range(halves):
                        rounded = jnp.concatenate([xs[place(f, c, r), :] for r in range(rows)], axis=0)
                        own[f, c] = rounded.astype(own.dtype)
            copy = pltpu.make_async_remote_copy(
                src_ref=own.at[first:last], dst_ref=halo.at[way, first:last],
                send_sem=own_sem.at[4 * turn], recv_sem=halo_recv.at[g],
                device_id={"reg": target}, device_id_type=MESH,
            )
            copy.start()

    loads[2].wait()
    block = n * pair
    j_row = lax.broadcasted_iota(jnp.int32, (block, everyone), 0)
    wanted = (j_row // pair) * members + lax.rem(j_row, members)
    chosen = lax.broadcasted_iota(jnp.int32, (block, everyone), 1) == wanted
    source = jnp.sum(
        jnp.where(chosen, jnp.broadcast_to(off_ref[...].astype(jnp.float32), (block, everyone)), 0.0),
        axis=1, keepdims=True,
    ).astype(jnp.int32)
    row = lax.broadcasted_iota(jnp.int32, (block, 1), 0)
    target_row = (source // members) * pair + lax.rem(row // members, rows) * members + lax.rem(source, members)
    k_col = lax.broadcasted_iota(jnp.int32, (block, block), 1)
    pick[...] = (k_col == jnp.broadcast_to(target_row, (block, block))).astype(jnp.float32).astype(pick.dtype)

    loads[3].wait()
    for c in range(halves):
        locs[c] = jnp.concatenate(
            [
                jnp.broadcast_to(loc_ref[r:r + 1, c * LANES:(c + 1) * LANES], (members, LANES))
                for r in range(rows)
            ],
            axis=0,
        )
    @pl.when(corner == 0)
    def _():
        pl.semaphore_wait(ready, 1)

    loads[1].wait()
    eye = lax.broadcasted_iota(jnp.int32, (members, members), 0) == lax.broadcasted_iota(
        jnp.int32, (members, members), 1
    )
    column = jnp.sum(jnp.where(eye, jnp.broadcast_to(w_ref[...], (members, members)), 0.0), axis=1, keepdims=True)
    wide[me] = jnp.broadcast_to(column, (members, LANES))
    for o in range(1, n):
        copy = pltpu.make_async_remote_copy(
            src_ref=wide.at[me], dst_ref=wide.at[me], send_sem=own_sem.at[1], recv_sem=w_recv,
            device_id={"mem": lax.rem(me + o, n)}, device_id_type=MESH,
        )
        copy.start()

    half = n // 2
    place_of_me = me * (1 - me // half) + (me // half) * (half + lax.rem(me + half - 2, half))

    def send(g, turns):
        first, last = groups[g]
        for d in turns:
            slot = d + (d - place_of_me + n) // n
            upper = slot // half
            peer = slot * (1 - upper) + upper * (half + lax.rem(slot + 2, half))
            copy = pltpu.make_async_remote_copy(
                src_ref=sendb.at[lax.rem(peer, halves), first:last], dst_ref=recv.at[me, first:last],
                send_sem=own_sem.at[2], recv_sem=to_recv.at[g],
                device_id={"mem": peer}, device_id_type=MESH,
            )
            copy.start()

    inner, outer = range(rows), range(-1, rows + 1)
    gains = []
    for g, (first, last) in enumerate(groups):
        settle(halo.at[:, first:last], halo_recv.at[g])

        def column_of(f):
            values = {}
            for way, base in ((0, -rows), (1, rows)):
                both = [halo[way, f, c].astype(jnp.float32) for c in range(halves)]
                for r in range(rows):
                    values[base + r] = jnp.concatenate([b[r * members:(r + 1) * members] for b in both], axis=1)
            for r in range(rows):
                values[r] = jnp.concatenate([xs[place(f, c, r), :] for c in range(halves)], axis=1)
            return values

        done = {}
        if g == 0:
            height, east, north = (column_of(f) for f in range(FLOWS))
            gains.append(tracer_gains(east, north, outer))
            flow = flow_step(height, east, north, outer)
            gains.append(tracer_gains(flow[1], flow[2], inner))
            for f, value in enumerate(flow_step(*flow, inner)):
                done[f] = value
        for f in range(max(first, FLOWS), last):
            done[f] = tracer_step(tracer_step(column_of(f), gains[0], outer), gains[1], inner)
        for f in range(first, last):
            for c in range(halves):
                both = jnp.concatenate([done[f][r][:, c * LANES:(c + 1) * LANES] for r in inner], axis=0)
                cast[f, c] = both
                sendb[c, f] = both.astype(sendb.dtype)
        send(g, range(n - 3))
        recv[me, first:last] = sendb[mine, first:last]
    for g in range(len(groups)):
        send(g, range(n - 3, n - 1))

    settle(wide.at[:n - 1], w_recv)
    weight = wide[...].reshape(n, 1, members, LANES)
    inverse = 1.0 / jnp.sum(jnp.sum(weight, axis=0), axis=1, keepdims=True)

    def posterior(copies, mean, ratio, local, forecast):
        return mean + ratio * (local * (copies - mean) + (1.0 - local) * (forecast - mean))

    local = locs[mine].reshape(1, rows, members, LANES)
    for g, (first, last) in enumerate(groups):
        settle(recv.at[:n - 1, first:last], to_recv.at[g])
        summary = {}
        for f in range(first, last):
            low_bits = recv[:, f].reshape(block, LANES)
            copies = lax.dot_general(
                pick[...], low_bits, (((1,), (0,)), ((), ())), preferred_element_type=jnp.float32
            )
            value = low_bits.astype(jnp.float32).reshape(n, rows, members, LANES)
            mean = jnp.sum(jnp.sum(weight * value, axis=0), axis=1, keepdims=True) * inverse
            departure = value - mean[None]
            variance = jnp.sum(jnp.sum(weight * departure * departure, axis=0), axis=1, keepdims=True) * inverse
            drawn = copies.reshape(n, rows, members, LANES)
            deviation = local * (drawn - mean[None]) + (1.0 - local) * departure
            spread = jnp.sum(jnp.sum(deviation * deviation, axis=0), axis=1, keepdims=True) / everyone
            ratio = jnp.sqrt((variance + small_eps) / (spread + small_eps))
            known = jnp.concatenate([mean[r] for r in range(rows)] + [ratio[r] for r in range(rows)], axis=0)
            coarse = known.astype(jnp.bfloat16).astype(jnp.float32)
            both = jnp.concatenate(
                [coarse, known - coarse, jnp.zeros((STATS - 4 * rows, LANES), jnp.float32)], axis=0
            ).astype(retb.dtype)
            kept[f] = copies.reshape(n, pair, LANES)
            retb[f, :pair] = kept[f, sibling].astype(retb.dtype)
            retb[f, pair:] = both
            summary[f] = mean, ratio
        copy = pltpu.make_async_remote_copy(
            src_ref=retb.at[first:last], dst_ref=got.at[first:last],
            send_sem=own_sem.at[3], recv_sem=halo_recv.at[g],
            device_id={"mem": sibling}, device_id_type=MESH,
        )
        copy.start()
        for f in range(first, last):
            mean, ratio = summary[f]
            wanted_here = kept[f, me]
            forecast = cast[f, mine]
            for r in range(rows):
                part = slice(r * members, (r + 1) * members)
                out_ref[place(f, mine, r), :] = posterior(
                    wanted_here[part], mean[r], ratio[r], locs[mine, part], forecast[part]
                )

    for g, (first, last) in enumerate(groups):
        settle(got.at[first:last], halo_recv.at[g])
        for f in range(first, last):
            block_in = got[f].astype(jnp.float32)
            known = block_in[pair:pair + 2 * rows] + block_in[pair + 2 * rows:pair + 4 * rows]
            forecast = cast[f, other]
            for r in range(rows):
                part = slice(r * members, (r + 1) * members)
                out_ref[place(f, other, r), :] = posterior(
                    block_in[part], known[r:r + 1], known[rows + r:rows + r + 1], locs[other, part], forecast[part]
                )

    @pl.when(last_band == 0)
    def _():
        settle(own, own_sem.at[0])

    for ref, i in ((own, 4), (wide.at[:n - 1], 1), (recv.at[:n - 1], 2), (retb, 3)):
        settle(ref, own_sem.at[i])


def solution(mesh):
    n, regs = mesh.shape["mem"], mesh.shape["reg"]

    def per_device(sample_stack, weights, offspring, localize):
        members, fields, rows, width = sample_stack.shape
        halves = width // LANES
        groups = field_groups(fields)
        count = len(groups)
        pair = rows * members
        x = sample_stack.reshape(members, fields, rows, halves, LANES).transpose(0, 1, 3, 2, 4)
        x = x.reshape(members * fields * halves * rows, LANES)
        hbm = pl.BlockSpec(memory_space=pltpu.HBM)
        vmem = pltpu.VMEM
        sem = pltpu.SemaphoreType.DMA
        f32, b16 = jnp.float32, jnp.bfloat16
        out = pl.pallas_call(
            functools.partial(kernel, n, regs, groups, fields, rows, halves, members),
            out_shape=jax.ShapeDtypeStruct(x.shape, f32),
            in_specs=[hbm] * 4,
            out_specs=pl.BlockSpec(memory_space=vmem),
            scratch_shapes=[
                vmem(x.shape, f32),
                vmem(weights.shape, f32),
                vmem(offspring.shape, jnp.int32),
                vmem(localize.shape, f32),
                vmem((fields, halves, pair, LANES), b16),
                vmem((2, fields, halves, pair, LANES), b16),
                vmem((fields, halves, pair, LANES), f32),
                vmem((halves, fields, pair, LANES), b16),
                vmem((n, fields, pair, LANES), b16),
                vmem((fields, pair + STATS, LANES), b16),
                vmem((fields, pair + STATS, LANES), b16),
                vmem((n, members, LANES), f32),
                vmem((halves, pair, LANES), f32),
                vmem((n * pair, n * pair), b16),
                vmem((fields, n, pair, LANES), f32),
                sem((5,)), sem((count,)), sem((count,)), sem,
                pltpu.SemaphoreType.REGULAR, pltpu.SemaphoreType.REGULAR,
            ],
            compiler_params=pltpu.CompilerParams(
                collective_id=0, has_side_effects=True, vmem_limit_bytes=32 << 20
            ),
        )(*(pltpu.with_memory_space_constraint(a, pltpu.HBM) for a in (x, weights, offspring, localize)))
        out = out.reshape(members, fields, halves, rows, LANES).transpose(0, 1, 3, 2, 4)
        return out.reshape(members, fields, rows, width)

    in_specs = (P("mem", None, "reg", None), P("reg", "mem"), P("reg", None), P("reg", None))
    return jax.shard_map(
        per_device, mesh=mesh, in_specs=in_specs, out_specs=P("mem", None, "reg", None), check_vma=False
    )
```

```python
import functools

import jax
import jax.numpy as jnp
from jax import lax
from jax.experimental import pallas as pl
from jax.experimental.pallas import tpu as pltpu
from jax.sharding import PartitionSpec as P

MESH = pl.DeviceIdType.MESH
wave_gain = 0.25
advect_gain = 0.1
diffuse_gain = 0.1
small_eps = 1e-05
LANES = 128
FLOWS = 3
STATS = 16


def field_groups(fields, sizes=(4, 4)):
    groups, first = [], 0
    for size in sizes + (fields,):
        last = min(fields, first + size)
        if last > first:
            groups.append((first, last))
        first = last
    return groups


def settle(ref, semaphore):
    pltpu.make_async_copy(ref, ref, semaphore).wait()


def sideways(block):
    width = block.shape[-1]
    return pltpu.roll(block, width - 1, 1), pltpu.roll(block, 1, 1)


def flow_step(height, east, north, rows):
    half = 0.5 * wave_gain
    new_height, new_east, new_north = {}, {}, {}
    for r in rows:
        e_right, e_left = sideways(east[r])
        h_right, h_left = sideways(height[r])
        new_height[r] = height[r] - half * ((e_right - e_left) + (north[r + 1] - north[r - 1]))
        new_east[r] = east[r] - half * (h_right - h_left)
        new_north[r] = north[r] - half * (height[r + 1] - height[r - 1])
    return new_height, new_east, new_north


def tracer_gains(east, north, rows):
    gains = {}
    for r in rows:
        e, v = (0.5 * advect_gain) * east[r], (0.5 * advect_gain) * north[r]
        gains[r] = (diffuse_gain - e, diffuse_gain + e, diffuse_gain - v, diffuse_gain + v)
    return gains


def tracer_step(tracer, gains, rows):
    new = {}
    for r in rows:
        right, left = sideways(tracer[r])
        g_right, g_left, g_up, g_low = gains[r]
        new[r] = (
            (1.0 - 4.0 * diffuse_gain) * tracer[r]
            + (g_right * right + g_left * left)
            + (g_up * tracer[r + 1] + g_low * tracer[r - 1])
        )
    return new


def kernel(
    n, regs, groups, fields, rows, halves, members,
    x_hbm, w_hbm, off_hbm, loc_hbm, out_ref,
    xs, w_ref, off_ref, loc_ref, own, halo, cast, sendb, recv, retb, got, wide, locs, pick, kept,
    own_sem, halo_recv, to_recv, w_recv, ready, go,
):
    me = lax.axis_index("mem")
    band = lax.axis_index("reg")
    stride = fields * halves * rows
    pair = rows * members
    everyone = n * members
    mine = lax.rem(me, halves)
    other = halves - 1 - mine
    sibling = me + other - mine

    loads = [
        pltpu.make_async_copy(src, dst, own_sem.at[i])
        for i, (src, dst) in enumerate(((x_hbm, xs), (w_hbm, w_ref), (off_hbm, off_ref), (loc_hbm, loc_ref)))
    ]
    loads[0].start()

    first_band = lax.rem(band + regs - 1, regs) // (regs - 1)
    second_band = lax.rem(band + regs - 2, regs) // (regs - 1)
    last_band = band // (regs - 1)
    corner = lax.rem(me + 1, n) // (n - 1)
    barrier = pltpu.get_barrier_semaphore()

    def greet(semaphore, **target):
        pl.semaphore_signal(semaphore, inc=1, device_id=target, device_id_type=MESH)

    @pl.when(corner == 0)
    def _():
        greet(barrier, mem=n - 2)

    @pl.when(last_band == 0)
    def _():
        greet(barrier, reg=band + 1)

    @pl.when(first_band + second_band == 1)
    def _():
        greet(barrier, reg=(regs - 1) * first_band)

    def place(f, c, r):
        return pl.ds((f * halves + c) * rows + r, members, stride=stride)

    pl.semaphore_wait(barrier, 1 + last_band + (n - 1) * corner)

    @pl.when(first_band + second_band == 0)
    def _():
        greet(go, reg=band - 1)

    @pl.when(last_band == 1)
    def _():
        greet(go, reg=0)

    loads[0].wait()
    up = first_band + last_band
    ways = (
        (lax.rem(band + 1 + (1 - up) * (regs - 2), regs), 1 - up),
        (lax.rem(band + 1 + up * (regs - 2), regs), up),
    )
    for turn, (target, way) in enumerate(ways):
        if turn == 1:
            for load in loads[1:]:
                load.start()

            @pl.when(corner == 1)
            def _():
                for d in (*range(n - 2), n - 1):
                    greet(ready, mem=d)

            @pl.when(last_band == 1)
            def _():
                settle(own, own_sem.at[0])

            @pl.when(last_band == 0)
            def _():
                pl.semaphore_wait(go, 1)

        for g, (first, last) in enumerate(groups):
            if turn == 0:
                for f in range(first, last):
                    for c in range(halves):
                        rounded = jnp.concatenate([xs[place(f, c, r), :] for r in range(rows)], axis=0)
                        own[f, c] = rounded.astype(own.dtype)
            copy = pltpu.make_async_remote_copy(
                src_ref=own.at[first:last], dst_ref=halo.at[way, first:last],
                send_sem=own_sem.at[4 * turn], recv_sem=halo_recv.at[g],
                device_id={"reg": target}, device_id_type=MESH,
            )
            copy.start()

    loads[2].wait()
    block = n * pair
    j_row = lax.broadcasted_iota(jnp.int32, (block, everyone), 0)
    wanted = (j_row // pair) * members + lax.rem(j_row, members)
    chosen = lax.broadcasted_iota(jnp.int32, (block, everyone), 1) == wanted
    source = jnp.sum(
        jnp.where(chosen, jnp.broadcast_to(off_ref[...].astype(jnp.float32), (block, everyone)), 0.0),
        axis=1, keepdims=True,
    ).astype(jnp.int32)
    row = lax.broadcasted_iota(jnp.int32, (block, 1), 0)
    target_row = (source // members) * pair + lax.rem(row // members, rows) * members + lax.rem(source, members)
    k_col = lax.broadcasted_iota(jnp.int32, (block, block), 1)
    pick[...] = (k_col == jnp.broadcast_to(target_row, (block, block))).astype(jnp.float32).astype(pick.dtype)

    loads[3].wait()
    for c in range(halves):
        locs[c] = jnp.concatenate(
            [
                jnp.broadcast_to(loc_ref[r:r + 1, c * LANES:(c + 1) * LANES], (members, LANES))
                for r in range(rows)
            ],
            axis=0,
        )
    @pl.when(corner == 0)
    def _():
        pl.semaphore_wait(ready, 1)

    loads[1].wait()
    eye = lax.broadcasted_iota(jnp.int32, (members, members), 0) == lax.broadcasted_iota(
        jnp.int32, (members, members), 1
    )
    column = jnp.sum(jnp.where(eye, jnp.broadcast_to(w_ref[...], (members, members)), 0.0), axis=1, keepdims=True)
    wide[me] = jnp.broadcast_to(column, (members, LANES))
    for o in range(1, n):
        copy = pltpu.make_async_remote_copy(
            src_ref=wide.at[me], dst_ref=wide.at[me], send_sem=own_sem.at[1], recv_sem=w_recv,
            device_id={"mem": lax.rem(me + o, n)}, device_id_type=MESH,
        )
        copy.start()

    half = n // 2
    place_of_me = me * (1 - me // half) + (me // half) * (half + lax.rem(me + half - 2, half))

    def send(g, turns):
        first, last = groups[g]
        for d in turns:
            slot = d + (d - place_of_me + n) // n
            upper = slot // half
            peer = slot * (1 - upper) + upper * (half + lax.rem(slot + 2, half))
            copy = pltpu.make_async_remote_copy(
                src_ref=sendb.at[lax.rem(peer, halves), first:last], dst_ref=recv.at[me, first:last],
                send_sem=own_sem.at[2], recv_sem=to_recv.at[g],
                device_id={"mem": peer}, device_id_type=MESH,
            )
            copy.start()

    inner, outer = range(rows), range(-1, rows + 1)
    gains = []
    for g, (first, last) in enumerate(groups):
        settle(halo.at[:, first:last], halo_recv.at[g])

        def column_of(f):
            values = {}
            for way, base in ((0, -rows), (1, rows)):
                both = [halo[way, f, c].astype(jnp.float32) for c in range(halves)]
                for r in range(rows):
                    values[base + r] = jnp.concatenate([b[r * members:(r + 1) * members] for b in both], axis=1)
            for r in range(rows):
                values[r] = jnp.concatenate([xs[place(f, c, r), :] for c in range(halves)], axis=1)
            return values

        done = {}
        if g == 0:
            height, east, north = (column_of(f) for f in range(FLOWS))
            gains.append(tracer_gains(east, north, outer))
            flow = flow_step(height, east, north, outer)
            gains.append(tracer_gains(flow[1], flow[2], inner))
            for f, value in enumerate(flow_step(*flow, inner)):
                done[f] = value
        for f in range(max(first, FLOWS), last):
            done[f] = tracer_step(tracer_step(column_of(f), gains[0], outer), gains[1], inner)
        for f in range(first, last):
            for c in range(halves):
                both = jnp.concatenate([done[f][r][:, c * LANES:(c + 1) * LANES] for r in inner], axis=0)
                cast[f, c] = both
                sendb[c, f] = both.astype(sendb.dtype)
        send(g, range(n - 3))
        recv[me, first:last] = sendb[mine, first:last]
    for g in range(len(groups)):
        send(g, range(n - 3, n - 1))

    settle(wide.at[:n - 1], w_recv)
    weight = wide[...].reshape(n, 1, members, LANES)
    inverse = 1.0 / jnp.sum(jnp.sum(weight, axis=0), axis=1, keepdims=True)

    def posterior(copies, mean, ratio, local, forecast):
        return mean + ratio * (local * (copies - mean) + (1.0 - local) * (forecast - mean))

    local = locs[mine].reshape(1, rows, members, LANES)
    for g, (first, last) in enumerate(groups):
        settle(recv.at[:n - 1, first:last], to_recv.at[g])
        summary = {}
        for f in range(first, last):
            low_bits = recv[:, f].reshape(block, LANES)
            copies = lax.dot_general(
                pick[...], low_bits, (((1,), (0,)), ((), ())), preferred_element_type=jnp.float32
            )
            value = low_bits.astype(jnp.float32).reshape(n, rows, members, LANES)
            mean = jnp.sum(jnp.sum(weight * value, axis=0), axis=1, keepdims=True) * inverse
            departure = value - mean[None]
            variance = jnp.sum(jnp.sum(weight * departure * departure, axis=0), axis=1, keepdims=True) * inverse
            drawn = copies.reshape(n, rows, members, LANES)
            deviation = local * (drawn - mean[None]) + (1.0 - local) * departure
            spread = jnp.sum(jnp.sum(deviation * deviation, axis=0), axis=1, keepdims=True) / everyone
            ratio = jnp.sqrt((variance + small_eps) / (spread + small_eps))
            known = jnp.concatenate([mean[r] for r in range(rows)] + [ratio[r] for r in range(rows)], axis=0)
            coarse = known.astype(jnp.bfloat16).astype(jnp.float32)
            both = jnp.concatenate(
                [coarse, known - coarse, jnp.zeros((STATS - 4 * rows, LANES), jnp.float32)], axis=0
            ).astype(retb.dtype)
            kept[f] = copies.reshape(n, pair, LANES)
            retb[f, :pair] = kept[f, sibling].astype(retb.dtype)
            retb[f, pair:] = both
            summary[f] = mean, ratio
        copy = pltpu.make_async_remote_copy(
            src_ref=retb.at[first:last], dst_ref=got.at[first:last],
            send_sem=own_sem.at[3], recv_sem=halo_recv.at[g],
            device_id={"mem": sibling}, device_id_type=MESH,
        )
        copy.start()
        for f in range(first, last):
            mean, ratio = summary[f]
            wanted_here = kept[f, me]
            forecast = cast[f, mine]
            for r in range(rows):
                part = slice(r * members, (r + 1) * members)
                out_ref[place(f, mine, r), :] = posterior(
                    wanted_here[part], mean[r], ratio[r], locs[mine, part], forecast[part]
                )

    @pl.when(last_band == 0)
    def _():
        settle(own, own_sem.at[0])

    for ref, i in ((own, 4), (wide.at[:n - 1], 1), (recv.at[:n - 1], 2)):
        settle(ref, own_sem.at[i])

    for g, (first, last) in enumerate(groups):
        settle(got.at[first:last], halo_recv.at[g])
        for f in range(first, last):
            block_in = got[f].astype(jnp.float32)
            known = block_in[pair:pair + 2 * rows] + block_in[pair + 2 * rows:pair + 4 * rows]
            forecast = cast[f, other]
            for r in range(rows):
                part = slice(r * members, (r + 1) * members)
                out_ref[place(f, other, r), :] = posterior(
                    block_in[part], known[r:r + 1], known[rows + r:rows + r + 1], locs[other, part], forecast[part]
                )

    settle(retb, own_sem.at[3])


def solution(mesh):
    n, regs = mesh.shape["mem"], mesh.shape["reg"]

    def per_device(sample_stack, weights, offspring, localize):
        members, fields, rows, width = sample_stack.shape
        halves = width // LANES
        groups = field_groups(fields)
        count = len(groups)
        pair = rows * members
        x = sample_stack.reshape(members, fields, rows, halves, LANES).transpose(0, 1, 3, 2, 4)
        x = x.reshape(members * fields * halves * rows, LANES)
        hbm = pl.BlockSpec(memory_space=pltpu.HBM)
        vmem = pltpu.VMEM
        sem = pltpu.SemaphoreType.DMA
        f32, b16 = jnp.float32, jnp.bfloat16
        out = pl.pallas_call(
            functools.partial(kernel, n, regs, groups, fields, rows, halves, members),
            out_shape=jax.ShapeDtypeStruct(x.shape, f32),
            in_specs=[hbm] * 4,
            out_specs=pl.BlockSpec(memory_space=vmem),
            scratch_shapes=[
                vmem(x.shape, f32),
                vmem(weights.shape, f32),
                vmem(offspring.shape, jnp.int32),
                vmem(localize.shape, f32),
                vmem((fields, halves, pair, LANES), b16),
                vmem((2, fields, halves, pair, LANES), b16),
                vmem((fields, halves, pair, LANES), f32),
                vmem((halves, fields, pair, LANES), b16),
                vmem((n, fields, pair, LANES), b16),
                vmem((fields, pair + STATS, LANES), b16),
                vmem((fields, pair + STATS, LANES), b16),
                vmem((n, members, LANES), f32),
                vmem((halves, pair, LANES), f32),
                vmem((n * pair, n * pair), b16),
                vmem((fields, n, pair, LANES), f32),
                sem((5,)), sem((count,)), sem((count,)), sem,
                pltpu.SemaphoreType.REGULAR, pltpu.SemaphoreType.REGULAR,
            ],
            compiler_params=pltpu.CompilerParams(
                collective_id=0, has_side_effects=True, vmem_limit_bytes=32 << 20
            ),
        )(*(pltpu.with_memory_space_constraint(a, pltpu.HBM) for a in (x, weights, offspring, localize)))
        out = out.reshape(members, fields, halves, rows, LANES).transpose(0, 1, 3, 2, 4)
        return out.reshape(members, fields, rows, width)

    in_specs = (P("mem", None, "reg", None), P("reg", "mem"), P("reg", None), P("reg", None))
    return jax.shard_map(
        per_device, mesh=mesh, in_specs=in_specs, out_specs=P("mem", None, "reg", None), check_vma=False
    )
```

```python
import functools

import jax
import jax.numpy as jnp
from jax import lax
from jax.experimental import pallas as pl
from jax.experimental.pallas import tpu as pltpu
from jax.sharding import PartitionSpec as P

MESH = pl.DeviceIdType.MESH
wave_gain = 0.25
advect_gain = 0.1
diffuse_gain = 0.1
small_eps = 1e-05
LANES = 128
FLOWS = 3
STATS = 16


def field_groups(fields, sizes=(5, 4)):
    groups, first = [], 0
    for size in sizes + (fields,):
        last = min(fields, first + size)
        if last > first:
            groups.append((first, last))
        first = last
    return groups


def settle(ref, semaphore):
    pltpu.make_async_copy(ref, ref, semaphore).wait()


def sideways(block):
    width = block.shape[-1]
    return pltpu.roll(block, width - 1, 1), pltpu.roll(block, 1, 1)


def flow_step(height, east, north, rows):
    half = 0.5 * wave_gain
    new_height, new_east, new_north = {}, {}, {}
    for r in rows:
        e_right, e_left = sideways(east[r])
        h_right, h_left = sideways(height[r])
        new_height[r] = height[r] - half * ((e_right - e_left) + (north[r + 1] - north[r - 1]))
        new_east[r] = east[r] - half * (h_right - h_left)
        new_north[r] = north[r] - half * (height[r + 1] - height[r - 1])
    return new_height, new_east, new_north


def tracer_gains(east, north, rows):
    gains = {}
    for r in rows:
        e, v = (0.5 * advect_gain) * east[r], (0.5 * advect_gain) * north[r]
        gains[r] = (diffuse_gain - e, diffuse_gain + e, diffuse_gain - v, diffuse_gain + v)
    return gains


def tracer_step(tracer, gains, rows):
    new = {}
    for r in rows:
        right, left = sideways(tracer[r])
        g_right, g_left, g_up, g_low = gains[r]
        new[r] = (
            (1.0 - 4.0 * diffuse_gain) * tracer[r]
            + (g_right * right + g_left * left)
            + (g_up * tracer[r + 1] + g_low * tracer[r - 1])
        )
    return new


def kernel(
    n, regs, groups, fields, rows, halves, members,
    x_hbm, w_hbm, off_hbm, loc_hbm, out_ref,
    xs, w_ref, off_ref, loc_ref, own, halo, cast, sendb, recv, retb, got, wide, locs, pick, kept,
    own_sem, halo_recv, to_recv, w_recv, ready, go,
):
    me = lax.axis_index("mem")
    band = lax.axis_index("reg")
    stride = fields * halves * rows
    pair = rows * members
    everyone = n * members
    mine = lax.rem(me, halves)
    other = halves - 1 - mine
    sibling = me + other - mine

    loads = [
        pltpu.make_async_copy(src, dst, own_sem.at[i])
        for i, (src, dst) in enumerate(((x_hbm, xs), (w_hbm, w_ref), (off_hbm, off_ref), (loc_hbm, loc_ref)))
    ]
    loads[0].start()

    first_band = lax.rem(band + regs - 1, regs) // (regs - 1)
    second_band = lax.rem(band + regs - 2, regs) // (regs - 1)
    last_band = band // (regs - 1)
    corner = lax.rem(me + 1, n) // (n - 1)
    barrier = pltpu.get_barrier_semaphore()

    def greet(semaphore, **target):
        pl.semaphore_signal(semaphore, inc=1, device_id=target, device_id_type=MESH)

    @pl.when(corner == 0)
    def _():
        greet(barrier, mem=n - 2)

    @pl.when(last_band == 0)
    def _():
        greet(barrier, reg=band + 1)

    @pl.when(first_band + second_band == 1)
    def _():
        greet(barrier, reg=(regs - 1) * first_band)

    def place(f, c, r):
        return pl.ds((f * halves + c) * rows + r, members, stride=stride)

    pl.semaphore_wait(barrier, 1 + last_band + (n - 1) * corner)

    @pl.when(first_band + second_band == 0)
    def _():
        greet(go, reg=band - 1)

    @pl.when(last_band == 1)
    def _():
        greet(go, reg=0)

    loads[0].wait()
    up = first_band + last_band
    ways = (
        (lax.rem(band + 1 + (1 - up) * (regs - 2), regs), 1 - up),
        (lax.rem(band + 1 + up * (regs - 2), regs), up),
    )
    for turn, (target, way) in enumerate(ways):
        if turn == 1:
            for load in loads[1:]:
                load.start()

            @pl.when(corner == 1)
            def _():
                for d in (*range(n - 2), n - 1):
                    greet(ready, mem=d)

            @pl.when(last_band == 1)
            def _():
                settle(own, own_sem.at[0])

            @pl.when(last_band == 0)
            def _():
                pl.semaphore_wait(go, 1)

        for g, (first, last) in enumerate(groups):
            if turn == 0:
                for f in range(first, last):
                    for c in range(halves):
                        rounded = jnp.concatenate([xs[place(f, c, r), :] for r in range(rows)], axis=0)
                        own[f, c] = rounded.astype(own.dtype)
            copy = pltpu.make_async_remote_copy(
                src_ref=own.at[first:last], dst_ref=halo.at[way, first:last],
                send_sem=own_sem.at[4 * turn], recv_sem=halo_recv.at[g],
                device_id={"reg": target}, device_id_type=MESH,
            )
            copy.start()

    loads[2].wait()
    block = n * pair
    j_row = lax.broadcasted_iota(jnp.int32, (block, everyone), 0)
    wanted = (j_row // pair) * members + lax.rem(j_row, members)
    chosen = lax.broadcasted_iota(jnp.int32, (block, everyone), 1) == wanted
    source = jnp.sum(
        jnp.where(chosen, jnp.broadcast_to(off_ref[...].astype(jnp.float32), (block, everyone)), 0.0),
        axis=1, keepdims=True,
    ).astype(jnp.int32)
    row = lax.broadcasted_iota(jnp.int32, (block, 1), 0)
    target_row = (source // members) * pair + lax.rem(row // members, rows) * members + lax.rem(source, members)
    k_col = lax.broadcasted_iota(jnp.int32, (block, block), 1)
    pick[...] = (k_col == jnp.broadcast_to(target_row, (block, block))).astype(jnp.float32).astype(pick.dtype)

    loads[3].wait()
    for c in range(halves):
        locs[c] = jnp.concatenate(
            [
                jnp.broadcast_to(loc_ref[r:r + 1, c * LANES:(c + 1) * LANES], (members, LANES))
                for r in range(rows)
            ],
            axis=0,
        )
    @pl.when(corner == 0)
    def _():
        pl.semaphore_wait(ready, 1)

    loads[1].wait()
    eye = lax.broadcasted_iota(jnp.int32, (members, members), 0) == lax.broadcasted_iota(
        jnp.int32, (members, members), 1
    )
    column = jnp.sum(jnp.where(eye, jnp.broadcast_to(w_ref[...], (members, members)), 0.0), axis=1, keepdims=True)
    wide[me] = jnp.broadcast_to(column, (members, LANES))
    for o in range(1, n):
        copy = pltpu.make_async_remote_copy(
            src_ref=wide.at[me], dst_ref=wide.at[me], send_sem=own_sem.at[1], recv_sem=w_recv,
            device_id={"mem": lax.rem(me + o, n)}, device_id_type=MESH,
        )
        copy.start()

    half = n // 2
    place_of_me = me * (1 - me // half) + (me // half) * (half + lax.rem(me + half - 2, half))

    def send(g, turns):
        first, last = groups[g]
        for d in turns:
            slot = d + (d - place_of_me + n) // n
            upper = slot // half
            peer = slot * (1 - upper) + upper * (half + lax.rem(slot + 2, half))
            copy = pltpu.make_async_remote_copy(
                src_ref=sendb.at[lax.rem(peer, halves), first:last], dst_ref=recv.at[me, first:last],
                send_sem=own_sem.at[2], recv_sem=to_recv.at[g],
                device_id={"mem": peer}, device_id_type=MESH,
            )
            copy.start()

    inner, outer = range(rows), range(-1, rows + 1)
    gains = []
    for g, (first, last) in enumerate(groups):
        settle(halo.at[:, first:last], halo_recv.at[g])

        def column_of(f):
            values = {}
            for way, base in ((0, -rows), (1, rows)):
                both = [halo[way, f, c].astype(jnp.float32) for c in range(halves)]
                for r in range(rows):
                    values[base + r] = jnp.concatenate([b[r * members:(r + 1) * members] for b in both], axis=1)
            for r in range(rows):
                values[r] = jnp.concatenate([xs[place(f, c, r), :] for c in range(halves)], axis=1)
            return values

        done = {}
        if g == 0:
            height, east, north = (column_of(f) for f in range(FLOWS))
            gains.append(tracer_gains(east, north, outer))
            flow = flow_step(height, east, north, outer)
            gains.append(tracer_gains(flow[1], flow[2], inner))
            for f, value in enumerate(flow_step(*flow, inner)):
                done[f] = value
        for f in range(max(first, FLOWS), last):
            done[f] = tracer_step(tracer_step(column_of(f), gains[0], outer), gains[1], inner)
        for f in range(first, last):
            for c in range(halves):
                both = jnp.concatenate([done[f][r][:, c * LANES:(c + 1) * LANES] for r in inner], axis=0)
                cast[f, c] = both
                sendb[c, f] = both.astype(sendb.dtype)
        send(g, range(n - 3))
        recv[me, first:last] = sendb[mine, first:last]
    for g in range(len(groups)):
        send(g, range(n - 3, n - 1))

    settle(wide.at[:n - 1], w_recv)
    weight = wide[...].reshape(n, 1, members, LANES)
    inverse = 1.0 / jnp.sum(jnp.sum(weight, axis=0), axis=1, keepdims=True)

    def posterior(copies, mean, ratio, local, forecast):
        return mean + ratio * (local * (copies - mean) + (1.0 - local) * (forecast - mean))

    local = locs[mine].reshape(1, rows, members, LANES)
    for g, (first, last) in enumerate(groups):
        settle(recv.at[:n - 1, first:last], to_recv.at[g])
        summary = {}
        for f in range(first, last):
            low_bits = recv[:, f].reshape(block, LANES)
            copies = lax.dot_general(
                pick[...], low_bits, (((1,), (0,)), ((), ())), preferred_element_type=jnp.float32
            )
            value = low_bits.astype(jnp.float32).reshape(n, rows, members, LANES)
            mean = jnp.sum(jnp.sum(weight * value, axis=0), axis=1, keepdims=True) * inverse
            departure = value - mean[None]
            variance = jnp.sum(jnp.sum(weight * departure * departure, axis=0), axis=1, keepdims=True) * inverse
            drawn = copies.reshape(n, rows, members, LANES)
            deviation = local * (drawn - mean[None]) + (1.0 - local) * departure
            spread = jnp.sum(jnp.sum(deviation * deviation, axis=0), axis=1, keepdims=True) / everyone
            ratio = jnp.sqrt((variance + small_eps) / (spread + small_eps))
            known = jnp.concatenate([mean[r] for r in range(rows)] + [ratio[r] for r in range(rows)], axis=0)
            coarse = known.astype(jnp.bfloat16).astype(jnp.float32)
            both = jnp.concatenate(
                [coarse, known - coarse, jnp.zeros((STATS - 4 * rows, LANES), jnp.float32)], axis=0
            ).astype(retb.dtype)
            kept[f] = copies.reshape(n, pair, LANES)
            retb[f, :pair] = kept[f, sibling].astype(retb.dtype)
            retb[f, pair:] = both
            summary[f] = mean, ratio
        copy = pltpu.make_async_remote_copy(
            src_ref=retb.at[first:last], dst_ref=got.at[first:last],
            send_sem=own_sem.at[3], recv_sem=halo_recv.at[g],
            device_id={"mem": sibling}, device_id_type=MESH,
        )
        copy.start()
        for f in range(first, last):
            mean, ratio = summary[f]
            wanted_here = kept[f, me]
            forecast = cast[f, mine]
            for r in range(rows):
                part = slice(r * members, (r + 1) * members)
                out_ref[place(f, mine, r), :] = posterior(
                    wanted_here[part], mean[r], ratio[r], locs[mine, part], forecast[part]
                )

    for g, (first, last) in enumerate(groups):
        settle(got.at[first:last], halo_recv.at[g])
        for f in range(first, last):
            block_in = got[f].astype(jnp.float32)
            known = block_in[pair:pair + 2 * rows] + block_in[pair + 2 * rows:pair + 4 * rows]
            forecast = cast[f, other]
            for r in range(rows):
                part = slice(r * members, (r + 1) * members)
                out_ref[place(f, other, r), :] = posterior(
                    block_in[part], known[r:r + 1], known[rows + r:rows + r + 1], locs[other, part], forecast[part]
                )

    @pl.when(last_band == 0)
    def _():
        settle(own, own_sem.at[0])

    for ref, i in ((own, 4), (wide.at[:n - 1], 1), (recv.at[:n - 1], 2), (retb, 3)):
        settle(ref, own_sem.at[i])


def solution(mesh):
    n, regs = mesh.shape["mem"], mesh.shape["reg"]

    def per_device(sample_stack, weights, offspring, localize):
        members, fields, rows, width = sample_stack.shape
        halves = width // LANES
        groups = field_groups(fields)
        count = len(groups)
        pair = rows * members
        x = sample_stack.reshape(members, fields, rows, halves, LANES).transpose(0, 1, 3, 2, 4)
        x = x.reshape(members * fields * halves * rows, LANES)
        hbm = pl.BlockSpec(memory_space=pltpu.HBM)
        vmem = pltpu.VMEM
        sem = pltpu.SemaphoreType.DMA
        f32, b16 = jnp.float32, jnp.bfloat16
        out = pl.pallas_call(
            functools.partial(kernel, n, regs, groups, fields, rows, halves, members),
            out_shape=jax.ShapeDtypeStruct(x.shape, f32),
            in_specs=[hbm] * 4,
            out_specs=pl.BlockSpec(memory_space=vmem),
            scratch_shapes=[
                vmem(x.shape, f32),
                vmem(weights.shape, f32),
                vmem(offspring.shape, jnp.int32),
                vmem(localize.shape, f32),
                vmem((fields, halves, pair, LANES), b16),
                vmem((2, fields, halves, pair, LANES), b16),
                vmem((fields, halves, pair, LANES), f32),
                vmem((halves, fields, pair, LANES), b16),
                vmem((n, fields, pair, LANES), b16),
                vmem((fields, pair + STATS, LANES), b16),
                vmem((fields, pair + STATS, LANES), b16),
                vmem((n, members, LANES), f32),
                vmem((halves, pair, LANES), f32),
                vmem((n * pair, n * pair), b16),
                vmem((fields, n, pair, LANES), f32),
                sem((5,)), sem((count,)), sem((count,)), sem,
                pltpu.SemaphoreType.REGULAR, pltpu.SemaphoreType.REGULAR,
            ],
            compiler_params=pltpu.CompilerParams(
                collective_id=0, has_side_effects=True, vmem_limit_bytes=32 << 20
            ),
        )(*(pltpu.with_memory_space_constraint(a, pltpu.HBM) for a in (x, weights, offspring, localize)))
        out = out.reshape(members, fields, halves, rows, LANES).transpose(0, 1, 3, 2, 4)
        return out.reshape(members, fields, rows, width)

    in_specs = (P("mem", None, "reg", None), P("reg", "mem"), P("reg", None), P("reg", None))
    return jax.shard_map(
        per_device, mesh=mesh, in_specs=in_specs, out_specs=P("mem", None, "reg", None), check_vma=False
    )
```
